512 devices in a mesh: seq: 32 (over x, y), chan: 16 (over z, core).
Axes of the slice: x: 4, y: 8, z: 8, core: 2. Of those that a mesh axis runs over, the one named last changes fastest.
Arguments:
- tokens: bfloat16 [1536, 16384], P('chan', 'seq'), may hold values from -6 to 6
- gate_weight: bfloat16 [1536, 1536], P('chan'), may hold values from -0.15625 to 0.15625
- value_weight: bfloat16 [1536, 1536], P('chan'), may hold values from -0.15625 to 0.15625
- first_factor: bfloat16 [64, 256, 256], P('seq'), may hold values from -0.375 to 0.375
- second_factor: bfloat16 [256, 64, 64], P('seq'), may hold values from -0.75 to 0.75
- down_latent: bfloat16 [1536, 128], P('chan'), may hold values from -0.15625 to 0.15625
- up_latent: bfloat16 [1536, 128], P('chan'), may hold values from -0.5 to 0.5
- doc_lengths: int32 [64], replicated, may hold values from 1 to 8704, 16384 in all
- cotangent: bfloat16 [1536, 16384], P('chan', 'seq'), may hold values from -6 to 6
Outputs:
- hidden: bfloat16 [1536, 16384], P('chan', 'seq')
- d_gate_weight: float32 [1536, 1536], P('chan')
- d_value_weight: float32 [1536, 1536], P('chan')
- d_first: float32 [64, 256, 256], P('seq', 'chan')
- d_second: float32 [256, 64, 64], P('seq', 'chan')
- d_down: float32 [1536, 128], P('chan')
- d_up: float32 [1536, 128], P('chan')
The draws below stay inside these ranges and needn't reach their ends.
Inputs may be any that keep to these rules, and one draw needn't show every extreme that they name: `doc_lengths`: the documents' lengths sum to 16384; the longest is exactly 8704 tokens.
All inputs are finite; a program needn't handle non-finite values.
Results may differ from the reference program's by a relative error of at most 0.0058.
Values may be sent and summed in bfloat16 or wider, within the bound.
No kernel may reach another device: no remote copies, remote signals or barrier semaphores. Data moves between devices by JAX's collectives and lax.ppermute only.
A program may use at most 64 MiB of HBM per device.

```python
import math
import jax
import jax.numpy as jnp
import numpy as np
from jax import lax

D = 1536
BLK = 256
LAT = 128
TOKENS = 16384
NB1 = 64
NDOC = 64
MOST = 8704


def shard_levels(rng, extent, shards, least, top_value):
    loudness, own = 1.0, jax.random.fold_in(rng, 6)
    for axis_at, blocks in shards:
        heights = jnp.exp(jax.random.uniform(jax.random.fold_in(own, axis_at), (blocks,), jnp.float32, least / len(shards), top_value / len(shards)))
        loudness = loudness * jnp.repeat(heights, extent[axis_at] // blocks).reshape([-1 if axis == axis_at else 1 for axis in range(len(extent))])
    return loudness


def profile(number_of, total, reach, slope):
    weights = [(1 << 20) // math.isqrt(grade ** slope) + 1 for grade in range(2, number_of + 1)]
    spare, given = total - reach - (number_of - 1), [1] * (number_of - 1)
    while spare > 0:
        free = [i for i in range(number_of - 1) if given[i] < reach]
        whole, left = sum([weights[i] for i in free]), spare
        for i in free:
            addition = min(reach - given[i], max(1, left * weights[i] // whole), spare)
            given[i] = given[i] + addition
            spare = spare - addition
    return np.array([reach] + given)


def ragged_sizes(own_key, amount, total, bound, lean):
    if amount == 2:
        one = jax.random.randint(own_key, (), max(1, total - bound), min(bound, total - 1) + 1)
        return jnp.stack([one, total - one])
    lengths = jnp.asarray(profile(amount, total, bound, lean), jnp.int32)
    twos = (amount - 1) // 2
    donor, sink = lengths[1:1 + 2 * twos:2], lengths[2:2 + 2 * twos:2]
    room = jnp.minimum(donor - 1, bound - sink)
    passed = jax.random.randint(jax.random.fold_in(own_key, 1), (twos,), 0, 1 << 20) % (room + 1)
    lengths = lengths.at[1:1 + 2 * twos:2].set(donor - passed).at[2:2 + 2 * twos:2].set(sink + passed)
    return lengths[jax.random.permutation(jax.random.fold_in(own_key, 2), amount)]


def noise(rng, shape, deviation, limit, cuts=(), kind=jnp.bfloat16):
    result = deviation * jax.random.normal(rng, shape, jnp.float32)
    if cuts:
        result = result * shard_levels(rng, shape, cuts, -0.22, 0.18)
    return jnp.clip(result, -limit, limit).astype(kind)


def setup_inputs(seed: int = 0) -> dict:
    key_list = jax.random.split(jax.random.key(seed), 10)
    tokens = noise(key_list[0], (D, TOKENS), 1.0, 6.0, ((0, 16), (1, 32)))
    gate_weight = noise(key_list[1], (D, D), D ** -0.5, 0.15625, ((0, 16),))
    value_weight = noise(key_list[2], (D, D), D ** -0.5, 0.15625, ((0, 16),))
    first_factor = noise(key_list[3], (NB1, BLK, BLK), BLK ** -0.5, 0.375, ((0, 32),))
    second_factor = noise(key_list[4], (BLK, NB1, NB1), NB1 ** -0.5, 0.75, ((0, 32),))
    down_latent = noise(key_list[5], (D, LAT), D ** -0.5, 0.15625, ((0, 16),))
    up_latent = noise(key_list[6], (D, LAT), LAT ** -0.5, 0.5, ((0, 16),))
    doc_lengths = ragged_sizes(key_list[7], NDOC, TOKENS, MOST, 2).astype(jnp.int32)
    cotangent = noise(key_list[8], (D, TOKENS), 1.0, 6.0, ((0, 16), (1, 32)))
    return {"tokens": tokens, "gate_weight": gate_weight, "value_weight": value_weight, "first_factor": first_factor, "second_factor": second_factor, "down_latent": down_latent, "up_latent": up_latent, "doc_lengths": doc_lengths, "cotangent": cotangent}


def reference(tokens, gate_weight, value_weight, first_factor, second_factor, down_latent, up_latent, doc_lengths, cotangent):
    highest = lax.Precision.HIGHEST
    inputs = tokens.T
    gate_w = gate_weight.T
    value_w = value_weight.T
    up_w = up_latent.T
    gate_pre = jnp.dot(inputs, gate_w, preferred_element_type=jnp.float32)
    value_bf = jnp.dot(inputs, value_w, preferred_element_type=jnp.float32).astype(jnp.bfloat16)
    doc_ends = jnp.cumsum(doc_lengths).astype(jnp.int32)
    doc_begins = (doc_ends - doc_lengths).astype(jnp.int32)
    position = jnp.arange(TOKENS, dtype=jnp.int32)
    member = ((position[:, None] >= doc_begins[None, :]) & (position[:, None] < doc_ends[None, :])).astype(jnp.float32)
    len_scale = lax.rsqrt(doc_lengths.astype(jnp.float32))
    latent = jnp.dot(inputs, down_latent, preferred_element_type=jnp.float32)
    pooled = jnp.dot(member.T, latent, precision=highest) * len_scale[:, None]
    spread = jnp.dot(pooled, up_w.astype(jnp.float32), precision=highest)
    summary = jnp.dot(member, spread, precision=highest)
    blocked = value_bf.reshape(NB1, BLK, D)
    inner_mix = jnp.einsum('ikj,ijc->ikc', first_factor.astype(jnp.float32), blocked.astype(jnp.float32)).astype(jnp.bfloat16)
    outer_mix = jnp.einsum('kmi,ikc->mkc', second_factor.astype(jnp.float32), inner_mix.astype(jnp.float32)).astype(jnp.bfloat16)
    mixed = outer_mix.reshape(TOKENS, D).astype(jnp.float32) + summary
    sig = jax.nn.sigmoid(gate_pre)
    act = gate_pre * sig
    hidden = (act * mixed).astype(jnp.bfloat16)
    upstream = cotangent.T.astype(jnp.float32)
    d_mixed = upstream * act
    d_mixed_bf = d_mixed.astype(jnp.bfloat16)
    d_gate_bf = (upstream * mixed * sig * (1.0 + gate_pre * (1.0 - sig))).astype(jnp.bfloat16)
    d_outer = d_mixed_bf.reshape(NB1, BLK, D).astype(jnp.float32)
    d_inner = jnp.einsum('kmi,mkc->ikc', second_factor.astype(jnp.float32), d_outer).astype(jnp.bfloat16)
    d_second = jnp.einsum('mkc,ikc->kmi', d_outer, inner_mix.astype(jnp.float32))
    d_value_bf = jnp.einsum('ikj,ikc->ijc', first_factor.astype(jnp.float32), d_inner.astype(jnp.float32)).astype(jnp.bfloat16).reshape(TOKENS, D)
    d_first = jnp.einsum('ikc,ijc->ikj', d_inner.astype(jnp.float32), blocked.astype(jnp.float32))
    per_doc = jnp.dot(member.T, d_mixed, precision=highest)
    d_up = jnp.dot(per_doc.T, pooled, precision=highest)
    d_pooled = jnp.dot(per_doc, up_w.astype(jnp.float32).T, precision=highest) * len_scale[:, None]
    d_latent_bf = jnp.dot(member, d_pooled, precision=highest).astype(jnp.bfloat16)
    d_down = jnp.dot(inputs.T, d_latent_bf, preferred_element_type=jnp.float32)
    d_gate_weight = jnp.dot(d_gate_bf.T, inputs, preferred_element_type=jnp.float32)
    d_value_weight = jnp.dot(d_value_bf.T, inputs, preferred_element_type=jnp.float32)
    return (hidden.T, d_gate_weight, d_value_weight, d_first, d_second, d_down, d_up)
```

```python
import jax
import jax.numpy as jnp
from jax import lax
from jax.sharding import PartitionSpec as P


HIGHEST = lax.Precision.HIGHEST


def seq_exchange(x):
    return lax.all_to_all(x, "seq", 0, 0, tiled=True)


def chan_exchange(x):
    return lax.all_to_all(x, "chan", 0, 0, tiled=True)


def body(
    tokens,
    gate_weight,
    value_weight,
    first_factor,
    second_factor,
    down_latent,
    up_latent,
    doc_lengths,
    cotangent,
):
    n_seq = lax.axis_size("seq")
    n_chan = lax.axis_size("chan")
    chan_rows, tok_cols = tokens.shape
    blocks_here, block_width, _ = first_factor.shape
    k_here, n_blk2, _ = second_factor.shape
    lat = down_latent.shape[1]
    n_doc = doc_lengths.shape[0]
    docs_here = n_doc // n_seq
    me = lax.axis_index("seq")

    packed = jnp.concatenate([tokens, down_latent], axis=1)
    gathered_all = lax.all_gather(packed, "chan", axis=0, tiled=True)
    gathered = gathered_all[:, :tok_cols]
    down_full = gathered_all[:, tok_cols:]

    doc_ends = jnp.cumsum(doc_lengths)
    doc_begins = doc_ends - doc_lengths
    position = me * tok_cols + jnp.arange(tok_cols, dtype=jnp.int32)
    member = (
        (position[None, :] >= doc_begins[:, None]) & (position[None, :] < doc_ends[:, None])
    ).astype(jnp.float32)
    len_scale = lax.rsqrt(doc_lengths.astype(jnp.float32))

    gate_pre = jnp.dot(gate_weight, gathered, preferred_element_type=jnp.float32)
    value_bf = jnp.dot(value_weight, gathered, preferred_element_type=jnp.float32).astype(
        jnp.bfloat16
    )
    latent = jnp.einsum("ct,cl->lt", gathered, down_full, preferred_element_type=jnp.float32)
    doc_lat_part = jnp.einsum("dt,lt->dl", member, latent, precision=HIGHEST)
    xdoc_part = jnp.einsum(
        "ct,dt->cd", tokens, member.astype(jnp.bfloat16), preferred_element_type=jnp.float32
    )

    blocked = value_bf.reshape(chan_rows, blocks_here, block_width)
    inner_mix = jnp.einsum(
        "ikj,cij->ikc", first_factor, blocked, preferred_element_type=jnp.float32
    ).astype(jnp.bfloat16)

    sig = jax.nn.sigmoid(gate_pre)
    act = gate_pre * sig
    upstream = cotangent.astype(jnp.float32)
    d_mixed = upstream * act
    d_mixed_bf = d_mixed.astype(jnp.bfloat16)
    per_doc_part = jnp.einsum("ct,dt->cd", d_mixed, member, precision=HIGHEST)

    inner_send = inner_mix.reshape(blocks_here, n_seq, k_here, chan_rows).transpose(1, 0, 2, 3)
    d_send = d_mixed_bf.reshape(chan_rows, blocks_here, n_seq, k_here).transpose(2, 1, 3, 0)
    recv2 = seq_exchange(jnp.concatenate([inner_send, d_send], axis=3))
    columns = recv2[..., :chan_rows].reshape(n_seq * blocks_here, k_here, chan_rows)
    d_outer = recv2[..., chan_rows:].reshape(n_seq * blocks_here, k_here, chan_rows)

    small_send = jnp.concatenate(
        [
            doc_lat_part.reshape(n_seq, docs_here * lat),
            per_doc_part.reshape(chan_rows, n_seq, docs_here)
            .transpose(1, 0, 2)
            .reshape(n_seq, chan_rows * docs_here),
            xdoc_part.reshape(chan_rows, n_seq, docs_here)
            .transpose(1, 0, 2)
            .reshape(n_seq, chan_rows * docs_here),
        ],
        axis=1,
    )
    small_red = jnp.sum(seq_exchange(small_send), axis=0)
    n_a = docs_here * lat
    n_b = chan_rows * docs_here
    scale_here = lax.dynamic_slice(len_scale, (me * docs_here,), (docs_here,))
    pooled_here = small_red[:n_a].reshape(docs_here, lat) * scale_here[:, None]
    per_doc_here = small_red[n_a : n_a + n_b].reshape(chan_rows, docs_here)
    xdoc_here = small_red[n_a + n_b :].reshape(chan_rows, docs_here)

    up_float = up_latent.astype(jnp.float32)
    g_part = jnp.einsum("cd,cl->dl", per_doc_here, up_float, precision=HIGHEST)
    g_here = jnp.sum(
        chan_exchange(jnp.broadcast_to(g_part.reshape(1, n_a), (n_chan, n_a))), axis=0
    )

    outer_mix = jnp.einsum(
        "kmi,ikc->mkc", second_factor, columns, preferred_element_type=jnp.float32
    ).astype(jnp.bfloat16)
    d_inner = jnp.einsum(
        "kmi,mkc->ikc", second_factor, d_outer, preferred_element_type=jnp.float32
    ).astype(jnp.bfloat16)
    d_second_part = jnp.einsum(
        "mkc,ikc->kmi", d_outer, columns, preferred_element_type=jnp.float32
    )

    outer_send = outer_mix.reshape(n_seq, blocks_here, k_here, chan_rows)
    dinner_send = d_inner.reshape(n_seq, blocks_here, k_here, chan_rows)
    recv3 = seq_exchange(jnp.concatenate([outer_send, dinner_send], axis=3))
    outer_tok = (
        recv3[..., :chan_rows].transpose(3, 1, 0, 2).reshape(chan_rows, tok_cols).astype(jnp.float32)
    )
    d_rows = recv3[..., chan_rows:].transpose(1, 0, 2, 3).reshape(
        blocks_here, n_seq * k_here, chan_rows
    )
    piece = jnp.concatenate(
        [pooled_here.reshape(n_a), per_doc_here.reshape(n_b), xdoc_here.reshape(n_b)]
    )
    gath3 = seq_exchange(jnp.broadcast_to(piece[None, :], (n_seq, piece.shape[0])))
    pooled = gath3[:, :n_a].reshape(n_doc, lat)
    per_doc = (
        gath3[:, n_a : n_a + n_b].reshape(n_seq, chan_rows, docs_here).transpose(1, 0, 2)
    ).reshape(chan_rows, n_doc)
    xdoc = (
        gath3[:, n_a + n_b :].reshape(n_seq, chan_rows, docs_here).transpose(1, 0, 2)
    ).reshape(chan_rows, n_doc)

    spread = jnp.einsum("dl,cl->cd", pooled, up_float, precision=HIGHEST)
    summary = jnp.dot(spread, member, precision=HIGHEST)
    mixed = outer_tok + summary
    hidden = (act * mixed).astype(jnp.bfloat16)
    d_gate_bf = (upstream * mixed * sig * (1.0 + gate_pre * (1.0 - sig))).astype(jnp.bfloat16)

    d_value_bf = (
        jnp.einsum("ikj,ikc->cij", first_factor, d_rows, preferred_element_type=jnp.float32)
        .astype(jnp.bfloat16)
        .reshape(chan_rows, tok_cols)
    )
    d_first_part = jnp.einsum("ikc,cij->ikj", d_rows, blocked, preferred_element_type=jnp.float32)
    d_up = jnp.einsum("cd,dl->cl", per_doc, pooled, precision=HIGHEST)

    both_grads = jnp.concatenate([d_gate_bf, d_value_bf], axis=0)
    d_proj_part = jnp.einsum("ot,it->oi", both_grads, gathered, preferred_element_type=jnp.float32)
    rows_here = 2 * chan_rows // n_seq
    width = d_proj_part.shape[1]

    proj_red = jnp.sum(seq_exchange(d_proj_part.reshape(n_seq, rows_here, width)), axis=0)
    k_part = block_width // n_chan
    m_part = n_blk2 // n_chan
    first_send = (
        d_first_part.reshape(blocks_here, n_chan, k_part, block_width)
        .transpose(1, 0, 2, 3)
        .reshape(n_chan, -1)
    )
    second_send = (
        d_second_part.reshape(k_here, n_chan, m_part, n_blk2).transpose(1, 0, 2, 3).reshape(n_chan, -1)
    )
    fac_red = jnp.sum(chan_exchange(jnp.concatenate([first_send, second_send], axis=1)), axis=0)
    n_f = blocks_here * k_part * block_width
    d_first = fac_red[:n_f].reshape(blocks_here, k_part, block_width)
    d_second = fac_red[n_f:].reshape(k_here, m_part, n_blk2)

    piece5 = jnp.concatenate([proj_red.reshape(-1), g_here])
    gath5 = seq_exchange(jnp.broadcast_to(piece5[None, :], (n_seq, piece5.shape[0])))
    n_p = rows_here * width
    d_proj = gath5[:, :n_p].reshape(2 * chan_rows, width)
    d_pooled = gath5[:, n_p:].reshape(n_doc, lat) * len_scale[:, None]
    d_down = jnp.einsum(
        "cd,dl->cl", xdoc, d_pooled.astype(jnp.bfloat16).astype(jnp.float32), precision=HIGHEST
    )
    return (hidden, d_proj[:chan_rows], d_proj[chan_rows:], d_first, d_second, d_down, d_up)


def solution(mesh):
    in_specs = (
        P("chan", "seq"),
        P("chan", None),
        P("chan", None),
        P("seq", None, None),
        P("seq", None, None),
        P("chan", None),
        P("chan", None),
        P(),
        P("chan", "seq"),
    )
    out_specs = (
        P("chan", "seq"),
        P("chan", None),
        P("chan", None),
        P("seq", "chan", None),
        P("seq", "chan", None),
        P("chan", None),
        P("chan", None),
    )
    return jax.shard_map(body, mesh=mesh, in_specs=in_specs, out_specs=out_specs, check_vma=False)
```

```python
import jax
import jax.numpy as jnp
from jax import lax
from jax.sharding import PartitionSpec as P


HIGHEST = lax.Precision.HIGHEST


def seq_exchange(x):
    return lax.all_to_all(x, "seq", 0, 0, tiled=True)


def chan_exchange(x):
    return lax.all_to_all(x, "chan", 0, 0, tiled=True)


def split_hi_lo(x):
    hi = x.astype(jnp.bfloat16)
    lo = (x - hi.astype(jnp.float32)).astype(jnp.bfloat16)
    return jnp.concatenate([hi, lo], axis=-1)


def join_hi_lo(x):
    n = x.shape[-1] // 2
    return x[..., :n].astype(jnp.float32) + x[..., n:].astype(jnp.float32)


def body(
    tokens,
    gate_weight,
    value_weight,
    first_factor,
    second_factor,
    down_latent,
    up_latent,
    doc_lengths,
    cotangent,
):
    n_seq = lax.axis_size("seq")
    n_chan = lax.axis_size("chan")
    chan_rows, tok_cols = tokens.shape
    blocks_here, block_width, _ = first_factor.shape
    k_here, n_blk2, _ = second_factor.shape
    lat = down_latent.shape[1]
    n_doc = doc_lengths.shape[0]
    docs_here = n_doc // n_seq
    me = lax.axis_index("seq")

    packed = jnp.concatenate([tokens, down_latent], axis=1)
    gathered_all = lax.all_gather(packed, "chan", axis=0, tiled=True)
    gathered = gathered_all[:, :tok_cols]
    down_full = gathered_all[:, tok_cols:]

    doc_ends = jnp.cumsum(doc_lengths)
    doc_begins = doc_ends - doc_lengths
    position = me * tok_cols + jnp.arange(tok_cols, dtype=jnp.int32)
    member = (
        (position[None, :] >= doc_begins[:, None]) & (position[None, :] < doc_ends[:, None])
    ).astype(jnp.float32)
    len_scale = lax.rsqrt(doc_lengths.astype(jnp.float32))

    gate_pre = jnp.dot(gate_weight, gathered, preferred_element_type=jnp.float32)
    value_bf = jnp.dot(value_weight, gathered, preferred_element_type=jnp.float32).astype(
        jnp.bfloat16
    )
    latent = jnp.einsum("ct,cl->lt", gathered, down_full, preferred_element_type=jnp.float32)
    doc_lat_part = jnp.einsum("dt,lt->dl", member, latent, precision=HIGHEST)
    xdoc_part = jnp.einsum(
        "ct,dt->cd", tokens, member.astype(jnp.bfloat16), preferred_element_type=jnp.float32
    )

    blocked = value_bf.reshape(chan_rows, blocks_here, block_width)
    inner_mix = jnp.einsum(
        "ikj,cij->ikc", first_factor, blocked, preferred_element_type=jnp.float32
    ).astype(jnp.bfloat16)

    sig = jax.nn.sigmoid(gate_pre)
    act = gate_pre * sig
    upstream = cotangent.astype(jnp.float32)
    d_mixed = upstream * act
    d_mixed_bf = d_mixed.astype(jnp.bfloat16)
    per_doc_part = jnp.einsum("ct,dt->cd", d_mixed, member, precision=HIGHEST)

    inner_send = inner_mix.reshape(blocks_here, n_seq, k_here, chan_rows).transpose(1, 0, 2, 3)
    d_send = d_mixed_bf.reshape(chan_rows, blocks_here, n_seq, k_here).transpose(2, 1, 3, 0)
    mix_send = jnp.concatenate([inner_send, d_send], axis=3).reshape(n_seq, -1)
    n_mix = mix_send.shape[1]

    small_send = jnp.concatenate(
        [
            doc_lat_part.reshape(n_seq, docs_here * lat),
            per_doc_part.reshape(chan_rows, n_seq, docs_here)
            .transpose(1, 0, 2)
            .reshape(n_seq, chan_rows * docs_here),
            xdoc_part.reshape(chan_rows, n_seq, docs_here)
            .transpose(1, 0, 2)
            .reshape(n_seq, chan_rows * docs_here),
        ],
        axis=1,
    )
    recv2 = seq_exchange(jnp.concatenate([mix_send, split_hi_lo(small_send)], axis=1))
    mix2 = recv2[:, :n_mix].reshape(n_seq, blocks_here, k_here, 2 * chan_rows)
    columns = mix2[..., :chan_rows].reshape(n_seq * blocks_here, k_here, chan_rows)
    d_outer = mix2[..., chan_rows:].reshape(n_seq * blocks_here, k_here, chan_rows)
    small_red = jnp.sum(join_hi_lo(recv2[:, n_mix:]), axis=0)
    n_a = docs_here * lat
    n_b = chan_rows * docs_here
    scale_here = lax.dynamic_slice(len_scale, (me * docs_here,), (docs_here,))
    pooled_here = small_red[:n_a].reshape(docs_here, lat) * scale_here[:, None]
    per_doc_here = small_red[n_a : n_a + n_b].reshape(chan_rows, docs_here)
    xdoc_here = small_red[n_a + n_b :].reshape(chan_rows, docs_here)

    up_float = up_latent.astype(jnp.float32)
    g_part = jnp.einsum("cd,cl->dl", per_doc_here, up_float, precision=HIGHEST)

    outer_mix = jnp.einsum(
        "kmi,ikc->mkc", second_factor, columns, preferred_element_type=jnp.float32
    ).astype(jnp.bfloat16)
    d_inner = jnp.einsum(
        "kmi,mkc->ikc", second_factor, d_outer, preferred_element_type=jnp.float32
    ).astype(jnp.bfloat16)
    d_second_part = jnp.einsum(
        "mkc,ikc->kmi", d_outer, columns, preferred_element_type=jnp.float32
    )

    outer_send = outer_mix.reshape(n_seq, blocks_here, k_here, chan_rows)
    dinner_send = d_inner.reshape(n_seq, blocks_here, k_here, chan_rows)
    piece = jnp.concatenate(
        [pooled_here.reshape(n_a), per_doc_here.reshape(n_b), xdoc_here.reshape(n_b)]
    )
    piece_b = jnp.broadcast_to(split_hi_lo(piece)[None, :], (n_seq, 2 * piece.shape[0]))
    send3 = jnp.concatenate(
        [jnp.concatenate([outer_send, dinner_send], axis=3).reshape(n_seq, -1), piece_b], axis=1
    )
    recv3_all = seq_exchange(send3)
    recv3 = recv3_all[:, :n_mix].reshape(n_seq, blocks_here, k_here, 2 * chan_rows)
    gath3 = join_hi_lo(recv3_all[:, n_mix:])
    outer_tok = (
        recv3[..., :chan_rows].transpose(3, 1, 0, 2).reshape(chan_rows, tok_cols).astype(jnp.float32)
    )
    d_rows = recv3[..., chan_rows:].transpose(1, 0, 2, 3).reshape(
        blocks_here, n_seq * k_here, chan_rows
    )
    pooled = gath3[:, :n_a].reshape(n_doc, lat)
    per_doc = (
        gath3[:, n_a : n_a + n_b].reshape(n_seq, chan_rows, docs_here).transpose(1, 0, 2)
    ).reshape(chan_rows, n_doc)
    xdoc = (
        gath3[:, n_a + n_b :].reshape(n_seq, chan_rows, docs_here).transpose(1, 0, 2)
    ).reshape(chan_rows, n_doc)

    spread = jnp.einsum("dl,cl->cd", pooled, up_float, precision=HIGHEST)
    summary = jnp.dot(spread, member, precision=HIGHEST)
    mixed = outer_tok + summary
    hidden = (act * mixed).astype(jnp.bfloat16)
    d_gate_bf = (upstream * mixed * sig * (1.0 + gate_pre * (1.0 - sig))).astype(jnp.bfloat16)

    d_value_bf = (
        jnp.einsum("ikj,ikc->cij", first_factor, d_rows, preferred_element_type=jnp.float32)
        .astype(jnp.bfloat16)
        .reshape(chan_rows, tok_cols)
    )
    d_first_part = jnp.einsum("ikc,cij->ikj", d_rows, blocked, preferred_element_type=jnp.float32)
    d_up = jnp.einsum("cd,dl->cl", per_doc, pooled, precision=HIGHEST)

    both_grads = jnp.concatenate([d_gate_bf, d_value_bf], axis=0)
    d_proj_part = jnp.einsum("ot,it->oi", both_grads, gathered, preferred_element_type=jnp.float32)
    rows_here = 2 * chan_rows // n_seq
    width = d_proj_part.shape[1]

    proj_red = jnp.sum(seq_exchange(d_proj_part.reshape(n_seq, rows_here, width)), axis=0)
    k_part = block_width // n_chan
    m_part = n_blk2 // n_chan
    first_send = (
        d_first_part.reshape(blocks_here, n_chan, k_part, block_width)
        .transpose(1, 0, 2, 3)
        .reshape(n_chan, -1)
    )
    second_send = (
        d_second_part.reshape(k_here, n_chan, m_part, n_blk2).transpose(1, 0, 2, 3).reshape(n_chan, -1)
    )
    g_send = jnp.broadcast_to(g_part.reshape(1, n_a), (n_chan, n_a))
    fac_red = jnp.sum(
        chan_exchange(jnp.concatenate([first_send, second_send, g_send], axis=1)), axis=0
    )
    n_f = blocks_here * k_part * block_width
    d_first = fac_red[:n_f].reshape(blocks_here, k_part, block_width)
    n_s = k_here * m_part * n_blk2
    d_second = fac_red[n_f : n_f + n_s].reshape(k_here, m_part, n_blk2)
    g_here = fac_red[n_f + n_s :]

    piece5 = jnp.concatenate([proj_red.reshape(-1), g_here])
    gath5 = seq_exchange(jnp.broadcast_to(piece5[None, :], (n_seq, piece5.shape[0])))
    n_p = rows_here * width
    d_proj = gath5[:, :n_p].reshape(2 * chan_rows, width)
    d_pooled = gath5[:, n_p:].reshape(n_doc, lat) * len_scale[:, None]
    d_down = jnp.einsum(
        "cd,dl->cl", xdoc, d_pooled.astype(jnp.bfloat16).astype(jnp.float32), precision=HIGHEST
    )
    return (hidden, d_proj[:chan_rows], d_proj[chan_rows:], d_first, d_second, d_down, d_up)


def solution(mesh):
    in_specs = (
        P("chan", "seq"),
        P("chan", None),
        P("chan", None),
        P("seq", None, None),
        P("seq", None, None),
        P("chan", None),
        P("chan", None),
        P(),
        P("chan", "seq"),
    )
    out_specs = (
        P("chan", "seq"),
        P("chan", None),
        P("chan", None),
        P("seq", "chan", None),
        P("seq", "chan", None),
        P("chan", None),
        P("chan", None),
    )
    return jax.shard_map(body, mesh=mesh, in_specs=in_specs, out_specs=out_specs, check_vma=False)
```

```python
import jax
import jax.numpy as jnp
from jax import lax
from jax.sharding import PartitionSpec as P


HIGHEST = lax.Precision.HIGHEST


def seq_exchange(x):
    return lax.all_to_all(x, "seq", 0, 0, tiled=True)


def chan_exchange(x):
    return lax.all_to_all(x, "chan", 0, 0, tiled=True)


def split_hi_lo(x):
    hi = lax.reduce_precision(x, exponent_bits=8, mantissa_bits=7)
    lo = x - hi
    return jnp.concatenate([hi.astype(jnp.bfloat16), lo.astype(jnp.bfloat16)], axis=-1)


def join_hi_lo(x):
    n = x.shape[-1] // 2
    return x[..., :n].astype(jnp.float32) + x[..., n:].astype(jnp.float32)


def body(
    tokens,
    gate_weight,
    value_weight,
    first_factor,
    second_factor,
    down_latent,
    up_latent,
    doc_lengths,
    cotangent,
):
    n_seq = lax.axis_size("seq")
    n_chan = lax.axis_size("chan")
    chan_rows, tok_cols = tokens.shape
    blocks_here, block_width, _ = first_factor.shape
    k_here, n_blk2, _ = second_factor.shape
    lat = down_latent.shape[1]
    n_doc = doc_lengths.shape[0]
    docs_here = n_doc // n_seq
    me = lax.axis_index("seq")

    packed = jnp.concatenate([tokens, down_latent], axis=1)
    gathered_all = lax.all_gather(packed, "chan", axis=0, tiled=True)
    gathered = gathered_all[:, :tok_cols]
    down_full = gathered_all[:, tok_cols:]

    doc_ends = jnp.cumsum(doc_lengths)
    doc_begins = doc_ends - doc_lengths
    position = me * tok_cols + jnp.arange(tok_cols, dtype=jnp.int32)
    member = (
        (position[None, :] >= doc_begins[:, None]) & (position[None, :] < doc_ends[:, None])
    ).astype(jnp.float32)
    len_scale = lax.rsqrt(doc_lengths.astype(jnp.float32))

    gate_pre = jnp.dot(gate_weight, gathered, preferred_element_type=jnp.float32)
    value_bf = jnp.dot(value_weight, gathered, preferred_element_type=jnp.float32).astype(
        jnp.bfloat16
    )
    latent = jnp.einsum("ct,cl->lt", gathered, down_full, preferred_element_type=jnp.float32)
    doc_lat_part = jnp.einsum("dt,lt->dl", member, latent, precision=HIGHEST)
    xdoc_part = jnp.einsum(
        "ct,dt->cd", tokens, member.astype(jnp.bfloat16), preferred_element_type=jnp.float32
    )

    blocked = value_bf.reshape(chan_rows, blocks_here, block_width)
    inner_mix = jnp.einsum(
        "ikj,cij->ikc", first_factor, blocked, preferred_element_type=jnp.float32
    ).astype(jnp.bfloat16)

    sig = jax.nn.sigmoid(gate_pre)
    act = gate_pre * sig
    upstream = cotangent.astype(jnp.float32)
    d_mixed = upstream * act
    d_mixed_bf = d_mixed.astype(jnp.bfloat16)
    per_doc_part = jnp.einsum("ct,dt->cd", d_mixed, member, precision=HIGHEST)

    inner_send = inner_mix.reshape(blocks_here, n_seq, k_here, chan_rows).transpose(1, 0, 2, 3)
    d_send = d_mixed_bf.reshape(chan_rows, blocks_here, n_seq, k_here).transpose(2, 1, 3, 0)
    mix_send = jnp.concatenate([inner_send, d_send], axis=3).reshape(n_seq, -1)
    n_mix = mix_send.shape[1]

    small_send = jnp.concatenate(
        [
            doc_lat_part.reshape(n_seq, docs_here * lat),
            per_doc_part.reshape(chan_rows, n_seq, docs_here)
            .transpose(1, 0, 2)
            .reshape(n_seq, chan_rows * docs_here),
            xdoc_part.reshape(chan_rows, n_seq, docs_here)
            .transpose(1, 0, 2)
            .reshape(n_seq, chan_rows * docs_here),
        ],
        axis=1,
    )
    recv2 = seq_exchange(jnp.concatenate([mix_send, split_hi_lo(small_send)], axis=1))
    mix2 = recv2[:, :n_mix].reshape(n_seq, blocks_here, k_here, 2 * chan_rows)
    columns = mix2[..., :chan_rows].reshape(n_seq * blocks_here, k_here, chan_rows)
    d_outer = mix2[..., chan_rows:].reshape(n_seq * blocks_here, k_here, chan_rows)
    small_red = jnp.sum(join_hi_lo(recv2[:, n_mix:]), axis=0)
    n_a = docs_here * lat
    n_b = chan_rows * docs_here
    scale_here = lax.dynamic_slice(len_scale, (me * docs_here,), (docs_here,))
    pooled_here = small_red[:n_a].reshape(docs_here, lat) * scale_here[:, None]
    per_doc_here = small_red[n_a : n_a + n_b].reshape(chan_rows, docs_here)
    xdoc_here = small_red[n_a + n_b :].reshape(chan_rows, docs_here)

    up_float = up_latent.astype(jnp.float32)
    g_part = jnp.einsum("cd,cl->dl", per_doc_here, up_float, precision=HIGHEST)

    outer_mix = jnp.einsum(
        "kmi,ikc->mkc", second_factor, columns, preferred_element_type=jnp.float32
    ).astype(jnp.bfloat16)
    d_inner = jnp.einsum(
        "kmi,mkc->ikc", second_factor, d_outer, preferred_element_type=jnp.float32
    ).astype(jnp.bfloat16)
    d_second_part = jnp.einsum(
        "mkc,ikc->kmi", d_outer, columns, preferred_element_type=jnp.float32
    )

    outer_send = outer_mix.reshape(n_seq, blocks_here, k_here, chan_rows)
    dinner_send = d_inner.reshape(n_seq, blocks_here, k_here, chan_rows)
    piece = jnp.concatenate(
        [pooled_here.reshape(n_a), per_doc_here.reshape(n_b), xdoc_here.reshape(n_b)]
    )
    piece_b = jnp.broadcast_to(split_hi_lo(piece)[None, :], (n_seq, 2 * piece.shape[0]))
    send3 = jnp.concatenate(
        [jnp.concatenate([outer_send, dinner_send], axis=3).reshape(n_seq, -1), piece_b], axis=1
    )
    recv3_all = seq_exchange(send3)
    recv3 = recv3_all[:, :n_mix].reshape(n_seq, blocks_here, k_here, 2 * chan_rows)
    gath3 = join_hi_lo(recv3_all[:, n_mix:])
    outer_tok = (
        recv3[..., :chan_rows].transpose(3, 1, 0, 2).reshape(chan_rows, tok_cols).astype(jnp.float32)
    )
    d_rows = recv3[..., chan_rows:].transpose(1, 0, 2, 3).reshape(
        blocks_here, n_seq * k_here, chan_rows
    )
    pooled = gath3[:, :n_a].reshape(n_doc, lat)
    per_doc = (
        gath3[:, n_a : n_a + n_b].reshape(n_seq, chan_rows, docs_here).transpose(1, 0, 2)
    ).reshape(chan_rows, n_doc)
    xdoc = (
        gath3[:, n_a + n_b :].reshape(n_seq, chan_rows, docs_here).transpose(1, 0, 2)
    ).reshape(chan_rows, n_doc)

    spread = jnp.einsum("dl,cl->cd", pooled, up_float, precision=HIGHEST)
    summary = jnp.dot(spread, member, precision=HIGHEST)
    mixed = outer_tok + summary
    hidden = (act * mixed).astype(jnp.bfloat16)
    d_gate_bf = (upstream * mixed * sig * (1.0 + gate_pre * (1.0 - sig))).astype(jnp.bfloat16)

    d_value_bf = (
        jnp.einsum("ikj,ikc->cij", first_factor, d_rows, preferred_element_type=jnp.float32)
        .astype(jnp.bfloat16)
        .reshape(chan_rows, tok_cols)
    )
    d_first_part = jnp.einsum("ikc,cij->ikj", d_rows, blocked, preferred_element_type=jnp.float32)
    d_up = jnp.einsum("cd,dl->cl", per_doc, pooled, precision=HIGHEST)

    both_grads = jnp.concatenate([d_gate_bf, d_value_bf], axis=0)
    d_proj_part = jnp.einsum("ot,it->oi", both_grads, gathered, preferred_element_type=jnp.float32)
    rows_here = 2 * chan_rows // n_seq
    width = d_proj_part.shape[1]

    proj_send = d_proj_part.reshape(n_seq, rows_here, width).astype(jnp.bfloat16)
    proj_red = jnp.sum(seq_exchange(proj_send).astype(jnp.float32), axis=0)
    k_part = block_width // n_chan
    m_part = n_blk2 // n_chan
    first_send = (
        d_first_part.reshape(blocks_here, n_chan, k_part, block_width)
        .transpose(1, 0, 2, 3)
        .reshape(n_chan, -1)
    )
    second_send = (
        d_second_part.reshape(k_here, n_chan, m_part, n_blk2).transpose(1, 0, 2, 3).reshape(n_chan, -1)
    )
    g_send = jnp.broadcast_to(g_part.reshape(1, n_a), (n_chan, n_a))
    fac_red = jnp.sum(
        chan_exchange(jnp.concatenate([first_send, second_send, g_send], axis=1)), axis=0
    )
    n_f = blocks_here * k_part * block_width
    d_first = fac_red[:n_f].reshape(blocks_here, k_part, block_width)
    n_s = k_here * m_part * n_blk2
    d_second = fac_red[n_f : n_f + n_s].reshape(k_here, m_part, n_blk2)
    g_here = fac_red[n_f + n_s :]

    piece5 = jnp.concatenate([proj_red.reshape(-1), g_here])
    gath5 = seq_exchange(jnp.broadcast_to(piece5[None, :], (n_seq, piece5.shape[0])))
    n_p = rows_here * width
    d_proj = gath5[:, :n_p].reshape(2 * chan_rows, width)
    d_pooled = gath5[:, n_p:].reshape(n_doc, lat) * len_scale[:, None]
    d_down = jnp.einsum(
        "cd,dl->cl", xdoc, d_pooled.astype(jnp.bfloat16).astype(jnp.float32), precision=HIGHEST
    )
    return (hidden, d_proj[:chan_rows], d_proj[chan_rows:], d_first, d_second, d_down, d_up)


def solution(mesh):
    in_specs = (
        P("chan", "seq"),
        P("chan", None),
        P("chan", None),
        P("seq", None, None),
        P("seq", None, None),
        P("chan", None),
        P("chan", None),
        P(),
        P("chan", "seq"),
    )
    out_specs = (
        P("chan", "seq"),
        P("chan", None),
        P("chan", None),
        P("seq", "chan", None),
        P("seq", "chan", None),
        P("chan", None),
        P("chan", None),
    )
    return jax.shard_map(body, mesh=mesh, in_specs=in_specs, out_specs=out_specs, check_vma=False)
```

```python
import jax
import jax.numpy as jnp
from jax import lax
from jax.sharding import PartitionSpec as P


HIGHEST = lax.Precision.HIGHEST


def seq_exchange(x):
    return lax.all_to_all(x, "seq", 0, 0, tiled=True)


def chan_exchange(x):
    return lax.all_to_all(x, "chan", 0, 0, tiled=True)


def split_hi_lo(x):
    hi = lax.reduce_precision(x, exponent_bits=8, mantissa_bits=7)
    lo = x - hi
    return jnp.concatenate([hi.astype(jnp.bfloat16), lo.astype(jnp.bfloat16)], axis=-1)


def join_hi_lo(x):
    n = x.shape[-1] // 2
    return x[..., :n].astype(jnp.float32) + x[..., n:].astype(jnp.float32)


def body(
    tokens,
    gate_weight,
    value_weight,
    first_factor,
    second_factor,
    down_latent,
    up_latent,
    doc_lengths,
    cotangent,
):
    n_seq = lax.axis_size("seq")
    n_chan = lax.axis_size("chan")
    chan_rows, tok_cols = tokens.shape
    blocks_here, block_width, _ = first_factor.shape
    k_here, n_blk2, _ = second_factor.shape
    lat = down_latent.shape[1]
    n_doc = doc_lengths.shape[0]
    docs_here = n_doc // n_seq
    me = lax.axis_index("seq")

    packed = jnp.concatenate([tokens, down_latent], axis=1)
    gathered_all = lax.all_gather(packed, "chan", axis=0, tiled=True)
    gathered = gathered_all[:, :tok_cols]
    down_full = gathered_all[:, tok_cols:]

    doc_ends = jnp.cumsum(doc_lengths)
    doc_begins = doc_ends - doc_lengths
    position = me * tok_cols + jnp.arange(tok_cols, dtype=jnp.int32)
    member = (
        (position[None, :] >= doc_begins[:, None]) & (position[None, :] < doc_ends[:, None])
    ).astype(jnp.float32)
    len_scale = lax.rsqrt(doc_lengths.astype(jnp.float32))

    gate_pre = jnp.dot(gate_weight, gathered, preferred_element_type=jnp.float32)
    value_bf = jnp.dot(value_weight, gathered, preferred_element_type=jnp.float32).astype(
        jnp.bfloat16
    )
    latent = jnp.einsum("ct,cl->lt", gathered, down_full, preferred_element_type=jnp.float32)
    doc_lat_part = jnp.einsum("dt,lt->dl", member, latent, precision=HIGHEST)
    xdoc_part = jnp.einsum(
        "ct,dt->cd", tokens, member.astype(jnp.bfloat16), preferred_element_type=jnp.float32
    )

    blocked = value_bf.reshape(chan_rows, blocks_here, block_width)
    inner_mix = jnp.einsum(
        "ikj,cij->ikc", first_factor, blocked, preferred_element_type=jnp.float32
    ).astype(jnp.bfloat16)

    sig = jax.nn.sigmoid(gate_pre)
    act = gate_pre * sig
    upstream = cotangent.astype(jnp.float32)
    d_mixed = upstream * act
    d_mixed_bf = d_mixed.astype(jnp.bfloat16)
    per_doc_part = jnp.einsum("ct,dt->cd", d_mixed, member, precision=HIGHEST)

    inner_send = inner_mix.reshape(blocks_here, n_seq, k_here, chan_rows).transpose(1, 0, 2, 3)
    d_send = d_mixed_bf.reshape(chan_rows, blocks_here, n_seq, k_here).transpose(2, 1, 3, 0)
    mix_send = jnp.concatenate([inner_send, d_send], axis=3).reshape(n_seq, -1)
    n_mix = mix_send.shape[1]

    small_send = jnp.concatenate(
        [
            doc_lat_part.reshape(n_seq, docs_here * lat),
            per_doc_part.reshape(chan_rows, n_seq, docs_here)
            .transpose(1, 0, 2)
            .reshape(n_seq, chan_rows * docs_here),
            xdoc_part.reshape(chan_rows, n_seq, docs_here)
            .transpose(1, 0, 2)
            .reshape(n_seq, chan_rows * docs_here),
        ],
        axis=1,
    )
    recv2 = seq_exchange(jnp.concatenate([mix_send, split_hi_lo(small_send)], axis=1))
    mix2 = recv2[:, :n_mix].reshape(n_seq, blocks_here, k_here, 2 * chan_rows)
    columns = mix2[..., :chan_rows].reshape(n_seq * blocks_here, k_here, chan_rows)
    d_outer = mix2[..., chan_rows:].reshape(n_seq * blocks_here, k_here, chan_rows)
    small_red = jnp.sum(join_hi_lo(recv2[:, n_mix:]), axis=0)
    n_a = docs_here * lat
    n_b = chan_rows * docs_here
    scale_here = lax.dynamic_slice(len_scale, (me * docs_here,), (docs_here,))
    pooled_here = small_red[:n_a].reshape(docs_here, lat) * scale_here[:, None]
    per_doc_here = small_red[n_a : n_a + n_b].reshape(chan_rows, docs_here)
    xdoc_here = small_red[n_a + n_b :].reshape(chan_rows, docs_here)

    up_float = up_latent.astype(jnp.float32)
    g_part = jnp.einsum("cd,cl->dl", per_doc_here, up_float, precision=HIGHEST)

    outer_mix = jnp.einsum(
        "kmi,ikc->mkc", second_factor, columns, preferred_element_type=jnp.float32
    ).astype(jnp.bfloat16)
    d_inner = jnp.einsum(
        "kmi,mkc->ikc", second_factor, d_outer, preferred_element_type=jnp.float32
    ).astype(jnp.bfloat16)
    d_second_part = jnp.einsum(
        "mkc,ikc->kmi", d_outer, columns, preferred_element_type=jnp.float32
    )

    outer_send = outer_mix.reshape(n_seq, blocks_here, k_here, chan_rows)
    dinner_send = d_inner.reshape(n_seq, blocks_here, k_here, chan_rows)
    piece = jnp.concatenate(
        [
            pooled_here.reshape(n_a),
            per_doc_here.reshape(n_b),
            xdoc_here.reshape(n_b),
            g_part.reshape(n_a),
        ]
    )
    piece_b = jnp.broadcast_to(split_hi_lo(piece)[None, :], (n_seq, 2 * piece.shape[0]))
    send3 = jnp.concatenate(
        [jnp.concatenate([outer_send, dinner_send], axis=3).reshape(n_seq, -1), piece_b], axis=1
    )
    recv3_all = seq_exchange(send3)
    recv3 = recv3_all[:, :n_mix].reshape(n_seq, blocks_here, k_here, 2 * chan_rows)
    gath3 = join_hi_lo(recv3_all[:, n_mix:])
    outer_tok = (
        recv3[..., :chan_rows].transpose(3, 1, 0, 2).reshape(chan_rows, tok_cols).astype(jnp.float32)
    )
    d_rows = recv3[..., chan_rows:].transpose(1, 0, 2, 3).reshape(
        blocks_here, n_seq * k_here, chan_rows
    )
    pooled = gath3[:, :n_a].reshape(n_doc, lat)
    per_doc = (
        gath3[:, n_a : n_a + n_b].reshape(n_seq, chan_rows, docs_here).transpose(1, 0, 2)
    ).reshape(chan_rows, n_doc)
    xdoc = (
        gath3[:, n_a + n_b : n_a + 2 * n_b].reshape(n_seq, chan_rows, docs_here).transpose(1, 0, 2)
    ).reshape(chan_rows, n_doc)
    g_gath = gath3[:, n_a + 2 * n_b :].reshape(1, n_doc * lat)

    spread = jnp.einsum("dl,cl->cd", pooled, up_float, precision=HIGHEST)
    summary = jnp.dot(spread, member, precision=HIGHEST)
    mixed = outer_tok + summary
    hidden = (act * mixed).astype(jnp.bfloat16)
    d_gate_bf = (upstream * mixed * sig * (1.0 + gate_pre * (1.0 - sig))).astype(jnp.bfloat16)

    d_value_bf = (
        jnp.einsum("ikj,ikc->cij", first_factor, d_rows, preferred_element_type=jnp.float32)
        .astype(jnp.bfloat16)
        .reshape(chan_rows, tok_cols)
    )
    d_first_part = jnp.einsum("ikc,cij->ikj", d_rows, blocked, preferred_element_type=jnp.float32)
    d_up = jnp.einsum("cd,dl->cl", per_doc, pooled, precision=HIGHEST)

    both_grads = jnp.concatenate([d_gate_bf, d_value_bf], axis=0)
    d_proj_part = jnp.einsum("ot,it->oi", both_grads, gathered, preferred_element_type=jnp.float32)
    rows_here = 2 * chan_rows // n_seq
    width = d_proj_part.shape[1]

    proj_send = d_proj_part.reshape(n_seq, rows_here, width).astype(jnp.bfloat16)
    proj_red = jnp.sum(seq_exchange(proj_send).astype(jnp.float32), axis=0)
    k_part = block_width // n_chan
    m_part = n_blk2 // n_chan
    first_send = (
        d_first_part.reshape(blocks_here, n_chan, k_part, block_width)
        .transpose(1, 0, 2, 3)
        .reshape(n_chan, -1)
    )
    second_send = (
        d_second_part.reshape(k_here, n_chan, m_part, n_blk2).transpose(1, 0, 2, 3).reshape(n_chan, -1)
    )
    g_send = jnp.broadcast_to(g_gath, (n_chan, n_doc * lat))
    fac_send = jnp.concatenate([first_send, second_send, g_send], axis=1)
    fac_red = lax.psum_scatter(
        fac_send.reshape(-1, 128), "chan", scatter_dimension=0, tiled=True
    ).reshape(-1)
    n_f = blocks_here * k_part * block_width
    d_first = fac_red[:n_f].reshape(blocks_here, k_part, block_width)
    n_s = k_here * m_part * n_blk2
    d_second = fac_red[n_f : n_f + n_s].reshape(k_here, m_part, n_blk2)
    g_full = fac_red[n_f + n_s :].reshape(n_doc, lat)

    gath5 = seq_exchange(jnp.broadcast_to(proj_red[None], (n_seq, rows_here, width)))
    d_proj = gath5.reshape(2 * chan_rows, width)
    d_pooled = g_full * len_scale[:, None]
    d_down = jnp.einsum(
        "cd,dl->cl", xdoc, d_pooled.astype(jnp.bfloat16).astype(jnp.float32), precision=HIGHEST
    )
    return (hidden, d_proj[:chan_rows], d_proj[chan_rows:], d_first, d_second, d_down, d_up)


def solution(mesh):
    in_specs = (
        P("chan", "seq"),
        P("chan", None),
        P("chan", None),
        P("seq", None, None),
        P("seq", None, None),
        P("chan", None),
        P("chan", None),
        P(),
        P("chan", "seq"),
    )
    out_specs = (
        P("chan", "seq"),
        P("chan", None),
        P("chan", None),
        P("seq", "chan", None),
        P("seq", "chan", None),
        P("chan", None),
        P("chan", None),
    )
    return jax.shard_map(body, mesh=mesh, in_specs=in_specs, out_specs=out_specs, check_vma=False)
```

```python
import jax
import jax.numpy as jnp
from jax import lax
from jax.sharding import PartitionSpec as P
from jax.experimental import pallas as pl
from jax.experimental.pallas import tpu as pltpu


HIGHEST = lax.Precision.HIGHEST


def seq_exchange(x):
    return lax.all_to_all(x, "seq", 0, 0, tiled=True)


def chan_exchange(x):
    return lax.all_to_all(x, "chan", 0, 0, tiled=True)


def split_hi_lo(x):
    hi = lax.reduce_precision(x, exponent_bits=8, mantissa_bits=7)
    lo = x - hi
    return jnp.concatenate([hi.astype(jnp.bfloat16), lo.astype(jnp.bfloat16)], axis=-1)


def join_hi_lo(x):
    n = x.shape[-1] // 2
    return x[..., :n].astype(jnp.float32) + x[..., n:].astype(jnp.float32)


def nt_dot(a, b, precision=None):
    return lax.dot_general(
        a, b, (((1,), (1,)), ((), ())), precision=precision, preferred_element_type=jnp.float32
    )


def stage1_kernel(x_ref, gw_ref, vw_ref, cot_ref, mem_ref, gate_ref, val_ref, dmix_ref, perdoc_ref, doclat_ref, mx_ref):
    tok = gate_ref.shape[1]
    xt = x_ref[:, :tok]
    down = x_ref[:, tok:].astype(jnp.float32)
    g = jnp.dot(gw_ref[...], xt, preferred_element_type=jnp.float32)
    v = jnp.dot(vw_ref[...], xt, preferred_element_type=jnp.float32)
    gate_ref[...] = g
    val_ref[...] = v.astype(jnp.bfloat16)
    sig = 1.0 / (1.0 + jnp.exp(-g))
    dm = cot_ref[...].astype(jnp.float32) * (g * sig)
    dmix_ref[...] = dm.astype(jnp.bfloat16)
    mem = mem_ref[...]
    perdoc_ref[...] = nt_dot(dm, mem, HIGHEST)
    mx = nt_dot(mem.astype(jnp.bfloat16), xt)
    mx_ref[...] = mx
    doclat_ref[...] = jnp.dot(mx, down, precision=HIGHEST, preferred_element_type=jnp.float32)


def stage1(gathered_all, gate_weight, value_weight, cotangent, member):
    rows, tok = cotangent.shape
    n_doc = member.shape[0]
    d_all = gathered_all.shape[0]
    lat = gathered_all.shape[1] - tok
    f32, bf16 = jnp.float32, jnp.bfloat16
    out_shape = (
        jax.ShapeDtypeStruct((rows, tok), f32),
        jax.ShapeDtypeStruct((rows, tok), bf16),
        jax.ShapeDtypeStruct((rows, tok), bf16),
        jax.ShapeDtypeStruct((rows, n_doc), f32),
        jax.ShapeDtypeStruct((n_doc, lat), f32),
        jax.ShapeDtypeStruct((n_doc, d_all), f32),
    )
    flops = 4 * rows * d_all * tok + 2 * n_doc * tok * d_all + 12 * rows * tok * n_doc + 12 * n_doc * d_all * lat
    nbytes = 2 * (gathered_all.size + gate_weight.size + value_weight.size + cotangent.size) + 4 * member.size
    nbytes += 8 * rows * tok + 4 * (rows * n_doc + n_doc * lat + n_doc * d_all)
    vmem = pl.BlockSpec(memory_space=pltpu.VMEM)
    return pl.pallas_call(
        stage1_kernel,
        out_shape=out_shape,
        in_specs=[vmem] * 5,
        out_specs=[vmem] * 6,
        cost_estimate=pl.CostEstimate(flops=flops, bytes_accessed=nbytes, transcendentals=rows * tok),
        compiler_params=pltpu.CompilerParams(vmem_limit_bytes=48 * 1024 * 1024),
    )(gathered_all, gate_weight, value_weight, cotangent, member)


def body(
    tokens,
    gate_weight,
    value_weight,
    first_factor,
    second_factor,
    down_latent,
    up_latent,
    doc_lengths,
    cotangent,
):
    n_seq = lax.axis_size("seq")
    n_chan = lax.axis_size("chan")
    chan_rows, tok_cols = tokens.shape
    blocks_here, block_width, _ = first_factor.shape
    k_here, n_blk2, _ = second_factor.shape
    lat = down_latent.shape[1]
    n_doc = doc_lengths.shape[0]
    docs_here = n_doc // n_seq
    me = lax.axis_index("seq")

    packed = jnp.concatenate([tokens, down_latent], axis=1)
    gathered_all = lax.all_gather(packed, "chan", axis=0, tiled=True)
    gathered = gathered_all[:, :tok_cols]

    doc_ends = jnp.cumsum(doc_lengths)
    doc_begins = doc_ends - doc_lengths
    position = me * tok_cols + jnp.arange(tok_cols, dtype=jnp.int32)
    member = (
        (position[None, :] >= doc_begins[:, None]) & (position[None, :] < doc_ends[:, None])
    ).astype(jnp.float32)
    len_scale = lax.rsqrt(doc_lengths.astype(jnp.float32))

    gate_pre, value_bf, d_mixed_bf, per_doc_part, doc_lat_part, mx = stage1(
        gathered_all, gate_weight, value_weight, cotangent, member
    )
    chan_me = lax.axis_index("chan")
    xdoc_part = lax.dynamic_slice_in_dim(mx, chan_me * chan_rows, chan_rows, axis=1).T

    blocked = value_bf.reshape(chan_rows, blocks_here, block_width)
    inner_mix = jnp.einsum(
        "ikj,cij->ikc", first_factor, blocked, preferred_element_type=jnp.float32
    ).astype(jnp.bfloat16)

    sig = jax.nn.sigmoid(gate_pre)
    act = gate_pre * sig
    upstream = cotangent.astype(jnp.float32)

    inner_send = inner_mix.reshape(blocks_here, n_seq, k_here, chan_rows).transpose(1, 0, 2, 3)
    d_send = d_mixed_bf.reshape(chan_rows, blocks_here, n_seq, k_here).transpose(2, 1, 3, 0)
    mix_send = jnp.concatenate([inner_send, d_send], axis=3).reshape(n_seq, -1)
    n_mix = mix_send.shape[1]

    small_send = jnp.concatenate(
        [
            doc_lat_part.reshape(n_seq, docs_here * lat),
            per_doc_part.reshape(chan_rows, n_seq, docs_here)
            .transpose(1, 0, 2)
            .reshape(n_seq, chan_rows * docs_here),
            xdoc_part.reshape(chan_rows, n_seq, docs_here)
            .transpose(1, 0, 2)
            .reshape(n_seq, chan_rows * docs_here),
        ],
        axis=1,
    )
    recv2 = seq_exchange(jnp.concatenate([mix_send, split_hi_lo(small_send)], axis=1))
    mix2 = recv2[:, :n_mix].reshape(n_seq, blocks_here, k_here, 2 * chan_rows)
    columns = mix2[..., :chan_rows].reshape(n_seq * blocks_here, k_here, chan_rows)
    d_outer = mix2[..., chan_rows:].reshape(n_seq * blocks_here, k_here, chan_rows)
    small_red = jnp.sum(join_hi_lo(recv2[:, n_mix:]), axis=0)
    n_a = docs_here * lat
    n_b = chan_rows * docs_here
    scale_here = lax.dynamic_slice(len_scale, (me * docs_here,), (docs_here,))
    pooled_here = small_red[:n_a].reshape(docs_here, lat) * scale_here[:, None]
    per_doc_here = small_red[n_a : n_a + n_b].reshape(chan_rows, docs_here)
    xdoc_here = small_red[n_a + n_b :].reshape(chan_rows, docs_here)

    up_float = up_latent.astype(jnp.float32)
    g_part = jnp.einsum("cd,cl->dl", per_doc_here, up_float, precision=HIGHEST)

    outer_mix = jnp.einsum(
        "kmi,ikc->mkc", second_factor, columns, preferred_element_type=jnp.float32
    ).astype(jnp.bfloat16)
    d_inner = jnp.einsum(
        "kmi,mkc->ikc", second_factor, d_outer, preferred_element_type=jnp.float32
    ).astype(jnp.bfloat16)
    d_second_part = jnp.einsum(
        "mkc,ikc->kmi", d_outer, columns, preferred_element_type=jnp.float32
    )

    outer_send = outer_mix.reshape(n_seq, blocks_here, k_here, chan_rows)
    dinner_send = d_inner.reshape(n_seq, blocks_here, k_here, chan_rows)
    piece = jnp.concatenate(
        [
            pooled_here.reshape(n_a),
            per_doc_here.reshape(n_b),
            xdoc_here.reshape(n_b),
            g_part.reshape(n_a),
        ]
    )
    piece_b = jnp.broadcast_to(split_hi_lo(piece)[None, :], (n_seq, 2 * piece.shape[0]))
    send3 = jnp.concatenate(
        [jnp.concatenate([outer_send, dinner_send], axis=3).reshape(n_seq, -1), piece_b], axis=1
    )
    recv3_all = seq_exchange(send3)
    recv3 = recv3_all[:, :n_mix].reshape(n_seq, blocks_here, k_here, 2 * chan_rows)
    gath3 = join_hi_lo(recv3_all[:, n_mix:])
    outer_tok = (
        recv3[..., :chan_rows].transpose(3, 1, 0, 2).reshape(chan_rows, tok_cols).astype(jnp.float32)
    )
    d_rows = recv3[..., chan_rows:].transpose(1, 0, 2, 3).reshape(
        blocks_here, n_seq * k_here, chan_rows
    )
    pooled = gath3[:, :n_a].reshape(n_doc, lat)
    per_doc = (
        gath3[:, n_a : n_a + n_b].reshape(n_seq, chan_rows, docs_here).transpose(1, 0, 2)
    ).reshape(chan_rows, n_doc)
    xdoc = (
        gath3[:, n_a + n_b : n_a + 2 * n_b].reshape(n_seq, chan_rows, docs_here).transpose(1, 0, 2)
    ).reshape(chan_rows, n_doc)
    g_gath = gath3[:, n_a + 2 * n_b :].reshape(1, n_doc * lat)

    spread = jnp.einsum("dl,cl->cd", pooled, up_float, precision=HIGHEST)
    summary = jnp.dot(spread, member, precision=HIGHEST)
    mixed = outer_tok + summary
    hidden = (act * mixed).astype(jnp.bfloat16)
    d_gate_bf = (upstream * mixed * sig * (1.0 + gate_pre * (1.0 - sig))).astype(jnp.bfloat16)

    d_value_bf = (
        jnp.einsum("ikj,ikc->cij", first_factor, d_rows, preferred_element_type=jnp.float32)
        .astype(jnp.bfloat16)
        .reshape(chan_rows, tok_cols)
    )
    d_first_part = jnp.einsum("ikc,cij->ikj", d_rows, blocked, preferred_element_type=jnp.float32)
    d_up = jnp.einsum("cd,dl->cl", per_doc, pooled, precision=HIGHEST)

    both_grads = jnp.concatenate([d_gate_bf, d_value_bf], axis=0)
    d_proj_part = jnp.einsum("ot,it->oi", both_grads, gathered, preferred_element_type=jnp.float32)
    rows_here = 2 * chan_rows // n_seq
    width = d_proj_part.shape[1]

    proj_send = d_proj_part.reshape(n_seq, rows_here, width).astype(jnp.bfloat16)
    proj_red = jnp.sum(seq_exchange(proj_send).astype(jnp.float32), axis=0)
    k_part = block_width // n_chan
    m_part = n_blk2 // n_chan
    first_send = (
        d_first_part.reshape(blocks_here, n_chan, k_part, block_width)
        .transpose(1, 0, 2, 3)
        .reshape(n_chan, -1)
    )
    second_send = (
        d_second_part.reshape(k_here, n_chan, m_part, n_blk2).transpose(1, 0, 2, 3).reshape(n_chan, -1)
    )
    g_send = jnp.broadcast_to(g_gath, (n_chan, n_doc * lat))
    fac_send = jnp.concatenate([first_send, second_send, g_send], axis=1)
    fac_red = lax.psum_scatter(
        fac_send.reshape(-1, 128), "chan", scatter_dimension=0, tiled=True
    ).reshape(-1)
    n_f = blocks_here * k_part * block_width
    d_first = fac_red[:n_f].reshape(blocks_here, k_part, block_width)
    n_s = k_here * m_part * n_blk2
    d_second = fac_red[n_f : n_f + n_s].reshape(k_here, m_part, n_blk2)
    g_full = fac_red[n_f + n_s :].reshape(n_doc, lat)

    gath5 = seq_exchange(jnp.broadcast_to(proj_red[None], (n_seq, rows_here, width)))
    d_proj = gath5.reshape(2 * chan_rows, width)
    d_pooled = g_full * len_scale[:, None]
    d_down = jnp.einsum(
        "cd,dl->cl", xdoc, d_pooled.astype(jnp.bfloat16).astype(jnp.float32), precision=HIGHEST
    )
    return (hidden, d_proj[:chan_rows], d_proj[chan_rows:], d_first, d_second, d_down, d_up)


def solution(mesh):
    in_specs = (
        P("chan", "seq"),
        P("chan", None),
        P("chan", None),
        P("seq", None, None),
        P("seq", None, None),
        P("chan", None),
        P("chan", None),
        P(),
        P("chan", "seq"),
    )
    out_specs = (
        P("chan", "seq"),
        P("chan", None),
        P("chan", None),
        P("seq", "chan", None),
        P("seq", "chan", None),
        P("chan", None),
        P("chan", None),
    )
    return jax.shard_map(body, mesh=mesh, in_specs=in_specs, out_specs=out_specs, check_vma=False)
```

```python
import jax
import jax.numpy as jnp
from jax import lax
from jax.sharding import PartitionSpec as P
from jax.experimental import pallas as pl
from jax.experimental.pallas import tpu as pltpu


HIGHEST = lax.Precision.HIGHEST


def seq_exchange(x):
    return lax.all_to_all(x, "seq", 0, 0, tiled=True)


def chan_exchange(x):
    return lax.all_to_all(x, "chan", 0, 0, tiled=True)


def split_hi_lo(x):
    hi = lax.reduce_precision(x, exponent_bits=8, mantissa_bits=7)
    lo = x - hi
    return jnp.concatenate([hi.astype(jnp.bfloat16), lo.astype(jnp.bfloat16)], axis=-1)


def join_hi_lo(x):
    n = x.shape[-1] // 2
    return x[..., :n].astype(jnp.float32) + x[..., n:].astype(jnp.float32)


def nt_dot(a, b, precision=None):
    return lax.dot_general(
        a, b, (((1,), (1,)), ((), ())), precision=precision, preferred_element_type=jnp.float32
    )


def stage1_kernel(
    x_hbm, gw_hbm, vw_hbm, cot_hbm, mem_hbm,
    gate_ref, val_ref, dmix_ref, perdoc_ref, doclat_ref, mx_ref,
    x_v, gw_v, vw_v, cot_v, mem_v, sems,
):
    tok = gate_ref.shape[1]
    half = x_v.shape[0] // 2
    copies = [
        pltpu.make_async_copy(gw_hbm, gw_v, sems.at[0]),
        pltpu.make_async_copy(x_hbm.at[pl.ds(0, half)], x_v.at[pl.ds(0, half)], sems.at[1]),
        pltpu.make_async_copy(x_hbm.at[pl.ds(half, half)], x_v.at[pl.ds(half, half)], sems.at[2]),
        pltpu.make_async_copy(vw_hbm, vw_v, sems.at[3]),
        pltpu.make_async_copy(cot_hbm, cot_v, sems.at[4]),
        pltpu.make_async_copy(mem_hbm, mem_v, sems.at[5]),
    ]
    for c in copies:
        c.start()
    copies[0].wait()
    copies[1].wait()
    g = jnp.dot(gw_v[:, :half], x_v[:half, :tok], preferred_element_type=jnp.float32)
    copies[2].wait()
    g = g + jnp.dot(gw_v[:, half:], x_v[half:, :tok], preferred_element_type=jnp.float32)
    gate_ref[...] = g
    copies[3].wait()
    xt = x_v[:, :tok]
    v = jnp.dot(vw_v[...], xt, preferred_element_type=jnp.float32)
    val_ref[...] = v.astype(jnp.bfloat16)
    sig = 1.0 / (1.0 + jnp.exp(-g))
    copies[4].wait()
    dm = cot_v[...].astype(jnp.float32) * (g * sig)
    dmix_ref[...] = dm.astype(jnp.bfloat16)
    copies[5].wait()
    mem = mem_v[...]
    perdoc_ref[...] = nt_dot(dm, mem, HIGHEST)
    mx = nt_dot(mem.astype(jnp.bfloat16), xt)
    mx_ref[...] = mx
    down = x_v[:, tok:].astype(jnp.float32)
    doclat_ref[...] = jnp.dot(mx, down, precision=HIGHEST, preferred_element_type=jnp.float32)


def stage1(gathered_all, gate_weight, value_weight, cotangent, member):
    rows, tok = cotangent.shape
    n_doc = member.shape[0]
    d_all = gathered_all.shape[0]
    lat = gathered_all.shape[1] - tok
    f32, bf16 = jnp.float32, jnp.bfloat16
    out_shape = (
        jax.ShapeDtypeStruct((rows, tok), f32),
        jax.ShapeDtypeStruct((rows, tok), bf16),
        jax.ShapeDtypeStruct((rows, tok), bf16),
        jax.ShapeDtypeStruct((rows, n_doc), f32),
        jax.ShapeDtypeStruct((n_doc, lat), f32),
        jax.ShapeDtypeStruct((n_doc, d_all), f32),
    )
    flops = 4 * rows * d_all * tok + 2 * n_doc * tok * d_all + 12 * rows * tok * n_doc + 12 * n_doc * d_all * lat
    nbytes = 2 * (gathered_all.size + gate_weight.size + value_weight.size + cotangent.size) + 4 * member.size
    nbytes += 8 * rows * tok + 4 * (rows * n_doc + n_doc * lat + n_doc * d_all)
    operands = (gathered_all, gate_weight, value_weight, cotangent, member)
    return pl.pallas_call(
        stage1_kernel,
        out_shape=out_shape,
        in_specs=[pl.BlockSpec(memory_space=pl.ANY)] * 5,
        out_specs=[pl.BlockSpec(memory_space=pltpu.VMEM)] * 6,
        scratch_shapes=[pltpu.VMEM(a.shape, a.dtype) for a in operands]
        + [pltpu.SemaphoreType.DMA((6,))],
        cost_estimate=pl.CostEstimate(flops=flops, bytes_accessed=nbytes, transcendentals=rows * tok),
    )(*operands)


def body(
    tokens,
    gate_weight,
    value_weight,
    first_factor,
    second_factor,
    down_latent,
    up_latent,
    doc_lengths,
    cotangent,
):
    n_seq = lax.axis_size("seq")
    n_chan = lax.axis_size("chan")
    chan_rows, tok_cols = tokens.shape
    blocks_here, block_width, _ = first_factor.shape
    k_here, n_blk2, _ = second_factor.shape
    lat = down_latent.shape[1]
    n_doc = doc_lengths.shape[0]
    docs_here = n_doc // n_seq
    me = lax.axis_index("seq")

    packed = jnp.concatenate([tokens, down_latent], axis=1)
    gathered_all = lax.all_gather(packed, "chan", axis=0, tiled=True)
    gathered = gathered_all[:, :tok_cols]

    doc_ends = jnp.cumsum(doc_lengths)
    doc_begins = doc_ends - doc_lengths
    position = me * tok_cols + jnp.arange(tok_cols, dtype=jnp.int32)
    member = (
        (position[None, :] >= doc_begins[:, None]) & (position[None, :] < doc_ends[:, None])
    ).astype(jnp.float32)
    len_scale = lax.rsqrt(doc_lengths.astype(jnp.float32))

    gate_pre, value_bf, d_mixed_bf, per_doc_part, doc_lat_part, mx = stage1(
        gathered_all, gate_weight, value_weight, cotangent, member
    )
    chan_me = lax.axis_index("chan")
    xdoc_part = lax.dynamic_slice_in_dim(mx, chan_me * chan_rows, chan_rows, axis=1).T

    blocked = value_bf.reshape(chan_rows, blocks_here, block_width)
    inner_mix = jnp.einsum(
        "ikj,cij->ikc", first_factor, blocked, preferred_element_type=jnp.float32
    ).astype(jnp.bfloat16)

    sig = jax.nn.sigmoid(gate_pre)
    act = gate_pre * sig
    upstream = cotangent.astype(jnp.float32)

    inner_send = inner_mix.reshape(blocks_here, n_seq, k_here, chan_rows).transpose(1, 0, 2, 3)
    d_send = d_mixed_bf.reshape(chan_rows, blocks_here, n_seq, k_here).transpose(2, 1, 3, 0)
    mix_send = jnp.concatenate([inner_send, d_send], axis=3).reshape(n_seq, -1)
    n_mix = mix_send.shape[1]

    small_send = jnp.concatenate(
        [
            doc_lat_part.reshape(n_seq, docs_here * lat),
            per_doc_part.reshape(chan_rows, n_seq, docs_here)
            .transpose(1, 0, 2)
            .reshape(n_seq, chan_rows * docs_here),
            xdoc_part.reshape(chan_rows, n_seq, docs_here)
            .transpose(1, 0, 2)
            .reshape(n_seq, chan_rows * docs_here),
        ],
        axis=1,
    )
    recv2 = seq_exchange(jnp.concatenate([mix_send, split_hi_lo(small_send)], axis=1))
    mix2 = recv2[:, :n_mix].reshape(n_seq, blocks_here, k_here, 2 * chan_rows)
    columns = mix2[..., :chan_rows].reshape(n_seq * blocks_here, k_here, chan_rows)
    d_outer = mix2[..., chan_rows:].reshape(n_seq * blocks_here, k_here, chan_rows)
    small_red = jnp.sum(join_hi_lo(recv2[:, n_mix:]), axis=0)
    n_a = docs_here * lat
    n_b = chan_rows * docs_here
    scale_here = lax.dynamic_slice(len_scale, (me * docs_here,), (docs_here,))
    pooled_here = small_red[:n_a].reshape(docs_here, lat) * scale_here[:, None]
    per_doc_here = small_red[n_a : n_a + n_b].reshape(chan_rows, docs_here)
    xdoc_here = small_red[n_a + n_b :].reshape(chan_rows, docs_here)

    up_float = up_latent.astype(jnp.float32)
    g_part = jnp.einsum("cd,cl->dl", per_doc_here, up_float, precision=HIGHEST)

    outer_mix = jnp.einsum(
        "kmi,ikc->mkc", second_factor, columns, preferred_element_type=jnp.float32
    ).astype(jnp.bfloat16)
    d_inner = jnp.einsum(
        "kmi,mkc->ikc", second_factor, d_outer, preferred_element_type=jnp.float32
    ).astype(jnp.bfloat16)
    d_second_part = jnp.einsum(
        "mkc,ikc->kmi", d_outer, columns, preferred_element_type=jnp.float32
    )

    outer_send = outer_mix.reshape(n_seq, blocks_here, k_here, chan_rows)
    dinner_send = d_inner.reshape(n_seq, blocks_here, k_here, chan_rows)
    piece = jnp.concatenate(
        [
            pooled_here.reshape(n_a),
            per_doc_here.reshape(n_b),
            xdoc_here.reshape(n_b),
            g_part.reshape(n_a),
        ]
    )
    piece_b = jnp.broadcast_to(split_hi_lo(piece)[None, :], (n_seq, 2 * piece.shape[0]))
    send3 = jnp.concatenate(
        [jnp.concatenate([outer_send, dinner_send], axis=3).reshape(n_seq, -1), piece_b], axis=1
    )
    recv3_all = seq_exchange(send3)
    recv3 = recv3_all[:, :n_mix].reshape(n_seq, blocks_here, k_here, 2 * chan_rows)
    gath3 = join_hi_lo(recv3_all[:, n_mix:])
    outer_tok = (
        recv3[..., :chan_rows].transpose(3, 1, 0, 2).reshape(chan_rows, tok_cols).astype(jnp.float32)
    )
    d_rows = recv3[..., chan_rows:].transpose(1, 0, 2, 3).reshape(
        blocks_here, n_seq * k_here, chan_rows
    )
    pooled = gath3[:, :n_a].reshape(n_doc, lat)
    per_doc = (
        gath3[:, n_a : n_a + n_b].reshape(n_seq, chan_rows, docs_here).transpose(1, 0, 2)
    ).reshape(chan_rows, n_doc)
    xdoc = (
        gath3[:, n_a + n_b : n_a + 2 * n_b].reshape(n_seq, chan_rows, docs_here).transpose(1, 0, 2)
    ).reshape(chan_rows, n_doc)
    g_gath = gath3[:, n_a + 2 * n_b :].reshape(1, n_doc * lat)

    spread = jnp.einsum("dl,cl->cd", pooled, up_float, precision=HIGHEST)
    summary = jnp.dot(spread, member, precision=HIGHEST)
    mixed = outer_tok + summary
    hidden = (act * mixed).astype(jnp.bfloat16)
    d_gate_bf = (upstream * mixed * sig * (1.0 + gate_pre * (1.0 - sig))).astype(jnp.bfloat16)

    d_value_bf = (
        jnp.einsum("ikj,ikc->cij", first_factor, d_rows, preferred_element_type=jnp.float32)
        .astype(jnp.bfloat16)
        .reshape(chan_rows, tok_cols)
    )
    d_first_part = jnp.einsum("ikc,cij->ikj", d_rows, blocked, preferred_element_type=jnp.float32)
    d_up = jnp.einsum("cd,dl->cl", per_doc, pooled, precision=HIGHEST)

    both_grads = jnp.concatenate([d_gate_bf, d_value_bf], axis=0)
    d_proj_part = jnp.einsum("ot,it->oi", both_grads, gathered, preferred_element_type=jnp.float32)
    rows_here = 2 * chan_rows // n_seq
    width = d_proj_part.shape[1]

    proj_send = d_proj_part.reshape(n_seq, rows_here, width).astype(jnp.bfloat16)
    proj_red = jnp.sum(seq_exchange(proj_send).astype(jnp.float32), axis=0)
    k_part = block_width // n_chan
    m_part = n_blk2 // n_chan
    first_send = (
        d_first_part.reshape(blocks_here, n_chan, k_part, block_width)
        .transpose(1, 0, 2, 3)
        .reshape(n_chan, -1)
    )
    second_send = (
        d_second_part.reshape(k_here, n_chan, m_part, n_blk2).transpose(1, 0, 2, 3).reshape(n_chan, -1)
    )
    g_send = jnp.broadcast_to(g_gath, (n_chan, n_doc * lat))
    fac_send = jnp.concatenate([first_send, second_send, g_send], axis=1)
    fac_red = lax.psum_scatter(
        fac_send.reshape(-1, 128), "chan", scatter_dimension=0, tiled=True
    ).reshape(-1)
    n_f = blocks_here * k_part * block_width
    d_first = fac_red[:n_f].reshape(blocks_here, k_part, block_width)
    n_s = k_here * m_part * n_blk2
    d_second = fac_red[n_f : n_f + n_s].reshape(k_here, m_part, n_blk2)
    g_full = fac_red[n_f + n_s :].reshape(n_doc, lat)

    gath5 = seq_exchange(jnp.broadcast_to(proj_red[None], (n_seq, rows_here, width)))
    d_proj = gath5.reshape(2 * chan_rows, width)
    d_pooled = g_full * len_scale[:, None]
    d_down = jnp.einsum(
        "cd,dl->cl", xdoc, d_pooled.astype(jnp.bfloat16).astype(jnp.float32), precision=HIGHEST
    )
    return (hidden, d_proj[:chan_rows], d_proj[chan_rows:], d_first, d_second, d_down, d_up)


def solution(mesh):
    in_specs = (
        P("chan", "seq"),
        P("chan", None),
        P("chan", None),
        P("seq", None, None),
        P("seq", None, None),
        P("chan", None),
        P("chan", None),
        P(),
        P("chan", "seq"),
    )
    out_specs = (
        P("chan", "seq"),
        P("chan", None),
        P("chan", None),
        P("seq", "chan", None),
        P("seq", "chan", None),
        P("chan", None),
        P("chan", None),
    )
    return jax.shard_map(body, mesh=mesh, in_specs=in_specs, out_specs=out_specs, check_vma=False)
```

```python
import jax
import jax.numpy as jnp
from jax import lax
from jax.sharding import PartitionSpec as P


HIGHEST = lax.Precision.HIGHEST


def seq_exchange(x):
    return lax.all_to_all(x, "seq", 0, 0, tiled=True)


def split_hi_lo(x):
    hi = lax.reduce_precision(x, exponent_bits=8, mantissa_bits=7)
    lo = x - hi
    return jnp.concatenate([hi.astype(jnp.bfloat16), lo.astype(jnp.bfloat16)], axis=-1)


def join_hi_lo(x):
    n = x.shape[-1] // 2
    return x[..., :n].astype(jnp.float32) + x[..., n:].astype(jnp.float32)


def body(
    tokens,
    gate_weight,
    value_weight,
    first_factor,
    second_factor,
    down_latent,
    up_latent,
    doc_lengths,
    cotangent,
):
    n_seq = lax.axis_size("seq")
    n_chan = lax.axis_size("chan")
    chan_rows, tok_cols = tokens.shape
    blocks_here, block_width, _ = first_factor.shape
    k_here, n_blk2, _ = second_factor.shape
    lat = down_latent.shape[1]
    n_doc = doc_lengths.shape[0]
    docs_here = n_doc // n_seq
    me = lax.axis_index("seq")

    packed = jnp.concatenate([tokens, down_latent], axis=1)
    gathered_all = lax.all_gather(packed, "chan", axis=0, tiled=True)
    gathered = gathered_all[:, :tok_cols]
    down_full = gathered_all[:, tok_cols:]

    doc_ends = jnp.cumsum(doc_lengths)
    doc_begins = doc_ends - doc_lengths
    position = me * tok_cols + jnp.arange(tok_cols, dtype=jnp.int32)
    member = (
        (position[None, :] >= doc_begins[:, None]) & (position[None, :] < doc_ends[:, None])
    ).astype(jnp.float32)
    len_scale = lax.rsqrt(doc_lengths.astype(jnp.float32))

    gate_pre = jnp.dot(gate_weight, gathered, preferred_element_type=jnp.float32)
    value_bf = jnp.dot(value_weight, gathered, preferred_element_type=jnp.float32).astype(
        jnp.bfloat16
    )
    latent = jnp.einsum("ct,cl->lt", gathered, down_full, preferred_element_type=jnp.float32)
    doc_lat_part = jnp.einsum("dt,lt->dl", member, latent, precision=HIGHEST)
    xdoc_part = jnp.einsum(
        "ct,dt->cd", tokens, member.astype(jnp.bfloat16), preferred_element_type=jnp.float32
    )

    blocked = value_bf.reshape(chan_rows, blocks_here, block_width)
    inner_mix = jnp.einsum(
        "ikj,cij->ikc", first_factor, blocked, preferred_element_type=jnp.float32
    ).astype(jnp.bfloat16)

    sig = jax.nn.sigmoid(gate_pre)
    act = gate_pre * sig
    upstream = cotangent.astype(jnp.float32)
    d_mixed = upstream * act
    d_mixed_bf = d_mixed.astype(jnp.bfloat16)
    per_doc_part = jnp.einsum("ct,dt->cd", d_mixed, member, precision=HIGHEST)

    inner_send = inner_mix.reshape(blocks_here, n_seq, k_here, chan_rows).transpose(1, 0, 2, 3)
    d_send = d_mixed_bf.reshape(chan_rows, blocks_here, n_seq, k_here).transpose(2, 1, 3, 0)
    mix_send = jnp.concatenate([inner_send, d_send], axis=3).reshape(n_seq, -1)
    n_mix = mix_send.shape[1]

    small_send = jnp.concatenate(
        [
            doc_lat_part.reshape(n_seq, docs_here * lat),
            per_doc_part.reshape(chan_rows, n_seq, docs_here)
            .transpose(1, 0, 2)
            .reshape(n_seq, chan_rows * docs_here),
            xdoc_part.reshape(chan_rows, n_seq, docs_here)
            .transpose(1, 0, 2)
            .reshape(n_seq, chan_rows * docs_here),
        ],
        axis=1,
    )
    recv2 = seq_exchange(jnp.concatenate([mix_send, split_hi_lo(small_send)], axis=1))
    mix2 = recv2[:, :n_mix].reshape(n_seq, blocks_here, k_here, 2 * chan_rows)
    columns = mix2[..., :chan_rows].reshape(n_seq * blocks_here, k_here, chan_rows)
    d_outer = mix2[..., chan_rows:].reshape(n_seq * blocks_here, k_here, chan_rows)
    small_red = jnp.sum(join_hi_lo(recv2[:, n_mix:]), axis=0)
    n_a = docs_here * lat
    n_b = chan_rows * docs_here
    scale_here = lax.dynamic_slice(len_scale, (me * docs_here,), (docs_here,))
    pooled_here = small_red[:n_a].reshape(docs_here, lat) * scale_here[:, None]
    per_doc_here = small_red[n_a : n_a + n_b].reshape(chan_rows, docs_here)
    xdoc_here = small_red[n_a + n_b :].reshape(chan_rows, docs_here)

    up_float = up_latent.astype(jnp.float32)
    g_part = jnp.einsum("cd,cl->dl", per_doc_here, up_float, precision=HIGHEST)

    outer_mix = jnp.einsum(
        "kmi,ikc->mkc", second_factor, columns, preferred_element_type=jnp.float32
    ).astype(jnp.bfloat16)
    d_inner = jnp.einsum(
        "kmi,mkc->ikc", second_factor, d_outer, preferred_element_type=jnp.float32
    ).astype(jnp.bfloat16)
    d_second_part = jnp.einsum(
        "mkc,ikc->kmi", d_outer, columns, preferred_element_type=jnp.float32
    )

    outer_send = outer_mix.reshape(n_seq, blocks_here, k_here, chan_rows)
    dinner_send = d_inner.reshape(n_seq, blocks_here, k_here, chan_rows)
    piece = jnp.concatenate(
        [
            pooled_here.reshape(n_a),
            per_doc_here.reshape(n_b),
            xdoc_here.reshape(n_b),
            g_part.reshape(n_a),
        ]
    )
    piece_b = jnp.broadcast_to(split_hi_lo(piece)[None, :], (n_seq, 2 * piece.shape[0]))
    send3 = jnp.concatenate(
        [jnp.concatenate([outer_send, dinner_send], axis=3).reshape(n_seq, -1), piece_b], axis=1
    )
    recv3_all = seq_exchange(send3)
    recv3 = recv3_all[:, :n_mix].reshape(n_seq, blocks_here, k_here, 2 * chan_rows)
    gath3 = join_hi_lo(recv3_all[:, n_mix:])
    outer_tok = (
        recv3[..., :chan_rows].transpose(3, 1, 0, 2).reshape(chan_rows, tok_cols).astype(jnp.float32)
    )
    d_rows = recv3[..., chan_rows:].transpose(1, 0, 2, 3).reshape(
        blocks_here, n_seq * k_here, chan_rows
    )
    pooled = gath3[:, :n_a].reshape(n_doc, lat)
    per_doc = (
        gath3[:, n_a : n_a + n_b].reshape(n_seq, chan_rows, docs_here).transpose(1, 0, 2)
    ).reshape(chan_rows, n_doc)
    xdoc = (
        gath3[:, n_a + n_b : n_a + 2 * n_b].reshape(n_seq, chan_rows, docs_here).transpose(1, 0, 2)
    ).reshape(chan_rows, n_doc)
    g_gath = gath3[:, n_a + 2 * n_b :].reshape(1, n_doc * lat)

    spread = jnp.einsum("dl,cl->cd", pooled, up_float, precision=HIGHEST)
    summary = jnp.dot(spread, member, precision=HIGHEST)
    mixed = outer_tok + summary
    hidden = (act * mixed).astype(jnp.bfloat16)
    d_gate_bf = (upstream * mixed * sig * (1.0 + gate_pre * (1.0 - sig))).astype(jnp.bfloat16)

    d_value_bf = (
        jnp.einsum("ikj,ikc->cij", first_factor, d_rows, preferred_element_type=jnp.float32)
        .astype(jnp.bfloat16)
        .reshape(chan_rows, tok_cols)
    )
    d_first_part = jnp.einsum("ikc,cij->ikj", d_rows, blocked, preferred_element_type=jnp.float32)
    d_up = jnp.einsum("cd,dl->cl", per_doc, pooled, precision=HIGHEST)

    both_grads = jnp.concatenate([d_gate_bf, d_value_bf], axis=0)
    d_proj_part = jnp.einsum("ot,it->oi", both_grads, gathered, preferred_element_type=jnp.float32)
    rows_here = 2 * chan_rows // n_seq
    width = d_proj_part.shape[1]

    proj_send = d_proj_part.reshape(n_seq, rows_here, width).astype(jnp.bfloat16)
    proj_red = jnp.sum(seq_exchange(proj_send).astype(jnp.float32), axis=0)
    k_part = block_width // n_chan
    m_part = n_blk2 // n_chan
    first_send = (
        d_first_part.reshape(blocks_here, n_chan, k_part, block_width)
        .transpose(1, 0, 2, 3)
        .reshape(n_chan, -1)
    )
    second_send = (
        d_second_part.reshape(k_here, n_chan, m_part, n_blk2).transpose(1, 0, 2, 3).reshape(n_chan, -1)
    )
    g_send = jnp.broadcast_to(g_gath, (n_chan, n_doc * lat))
    fac_send = jnp.concatenate([first_send, second_send, g_send], axis=1)
    fac_red = lax.psum_scatter(fac_send.reshape(-1, 128), "chan", scatter_dimension=0, tiled=True)
    fac_red = fac_red.reshape(-1)
    n_f = blocks_here * k_part * block_width
    d_first = fac_red[:n_f].reshape(blocks_here, k_part, block_width)
    n_s = k_here * m_part * n_blk2
    d_second = fac_red[n_f : n_f + n_s].reshape(k_here, m_part, n_blk2)
    g_full = fac_red[n_f + n_s :].reshape(n_doc, lat)

    gath5 = seq_exchange(jnp.broadcast_to(proj_red[None], (n_seq, rows_here, width)))
    d_proj = gath5.reshape(2 * chan_rows, width)
    d_pooled = g_full * len_scale[:, None]
    d_down = jnp.einsum(
        "cd,dl->cl", xdoc, d_pooled.astype(jnp.bfloat16).astype(jnp.float32), precision=HIGHEST
    )
    return (hidden, d_proj[:chan_rows], d_proj[chan_rows:], d_first, d_second, d_down, d_up)


def solution(mesh):
    in_specs = (
        P("chan", "seq"),
        P("chan", None),
        P("chan", None),
        P("seq", None, None),
        P("seq", None, None),
        P("chan", None),
        P("chan", None),
        P(),
        P("chan", "seq"),
    )
    out_specs = (
        P("chan", "seq"),
        P("chan", None),
        P("chan", None),
        P("seq", "chan", None),
        P("seq", "chan", None),
        P("chan", None),
        P("chan", None),
    )

    return jax.shard_map(body, mesh=mesh, in_specs=in_specs, out_specs=out_specs, check_vma=False)
```

```python
import jax
import jax.numpy as jnp
from jax import lax
from jax.sharding import PartitionSpec as P


HIGHEST = lax.Precision.HIGHEST


def seq_exchange(x):
    return lax.all_to_all(x, "seq", 0, 0, tiled=True)


def split_hi_lo(x):
    hi = lax.reduce_precision(x, exponent_bits=8, mantissa_bits=7)
    lo = x - hi
    return jnp.concatenate([hi.astype(jnp.bfloat16), lo.astype(jnp.bfloat16)], axis=-1)


def join_hi_lo(x):
    n = x.shape[-1] // 2
    return x[..., :n].astype(jnp.float32) + x[..., n:].astype(jnp.float32)


def body(
    tokens,
    gate_weight,
    value_weight,
    first_factor,
    second_factor,
    down_latent,
    up_latent,
    doc_lengths,
    cotangent,
):
    n_seq = lax.axis_size("seq")
    n_chan = lax.axis_size("chan")
    chan_rows, tok_cols = tokens.shape
    blocks_here, block_width, _ = first_factor.shape
    k_here, n_blk2, _ = second_factor.shape
    lat = down_latent.shape[1]
    n_doc = doc_lengths.shape[0]
    docs_here = n_doc // n_seq
    me = lax.axis_index("seq")

    packed = jnp.concatenate([tokens, down_latent], axis=1)
    gathered_all = lax.all_gather(packed, "chan", axis=0, tiled=True)
    gathered = gathered_all[:, :tok_cols]
    down_full = gathered_all[:, tok_cols:]

    doc_ends = jnp.cumsum(doc_lengths)
    doc_begins = doc_ends - doc_lengths
    position = me * tok_cols + jnp.arange(tok_cols, dtype=jnp.int32)
    member = (
        (position[None, :] >= doc_begins[:, None]) & (position[None, :] < doc_ends[:, None])
    ).astype(jnp.float32)
    len_scale = lax.rsqrt(doc_lengths.astype(jnp.float32))

    gate_pre = jnp.dot(gate_weight, gathered, preferred_element_type=jnp.float32)
    value_bf = jnp.dot(value_weight, gathered, preferred_element_type=jnp.float32).astype(
        jnp.bfloat16
    )
    latent = jnp.einsum("ct,cl->lt", gathered, down_full, preferred_element_type=jnp.float32)
    doc_lat_part = jnp.einsum("dt,lt->dl", member, latent, precision=HIGHEST)
    xdoc_part = jnp.einsum(
        "ct,dt->cd", tokens, member.astype(jnp.bfloat16), preferred_element_type=jnp.float32
    )

    blocked = value_bf.reshape(chan_rows, blocks_here, block_width)
    inner_mix = jnp.einsum(
        "ikj,cij->ikc", first_factor, blocked, preferred_element_type=jnp.float32
    ).astype(jnp.bfloat16)

    sig = jax.nn.sigmoid(gate_pre)
    act = gate_pre * sig
    upstream = cotangent.astype(jnp.float32)
    d_mixed = upstream * act
    d_mixed_bf = d_mixed.astype(jnp.bfloat16)
    per_doc_part = jnp.einsum("ct,dt->cd", d_mixed, member, precision=HIGHEST)

    inner_send = inner_mix.reshape(blocks_here, n_seq, k_here, chan_rows).transpose(1, 0, 2, 3)
    d_send = d_mixed_bf.reshape(chan_rows, blocks_here, n_seq, k_here).transpose(2, 1, 3, 0)
    mix_send = jnp.concatenate([inner_send, d_send], axis=3).reshape(n_seq, -1)
    n_mix = mix_send.shape[1]

    small_send = jnp.concatenate(
        [
            doc_lat_part.reshape(n_seq, docs_here * lat),
            per_doc_part.reshape(chan_rows, n_seq, docs_here)
            .transpose(1, 0, 2)
            .reshape(n_seq, chan_rows * docs_here),
            xdoc_part.reshape(chan_rows, n_seq, docs_here)
            .transpose(1, 0, 2)
            .reshape(n_seq, chan_rows * docs_here),
        ],
        axis=1,
    )
    recv2 = seq_exchange(jnp.concatenate([mix_send, split_hi_lo(small_send)], axis=1))
    mix2 = recv2[:, :n_mix].reshape(n_seq, blocks_here, k_here, 2 * chan_rows)
    columns = mix2[..., :chan_rows].reshape(n_seq * blocks_here, k_here, chan_rows)
    d_outer = mix2[..., chan_rows:].reshape(n_seq * blocks_here, k_here, chan_rows)
    small_red = jnp.sum(join_hi_lo(recv2[:, n_mix:]), axis=0)
    n_a = docs_here * lat
    n_b = chan_rows * docs_here
    scale_here = lax.dynamic_slice(len_scale, (me * docs_here,), (docs_here,))
    pooled_here = small_red[:n_a].reshape(docs_here, lat) * scale_here[:, None]
    per_doc_here = small_red[n_a : n_a + n_b].reshape(chan_rows, docs_here)
    xdoc_here = small_red[n_a + n_b :].reshape(chan_rows, docs_here)

    up_float = up_latent.astype(jnp.float32)
    g_part = jnp.einsum("cd,cl->dl", per_doc_here, up_float, precision=HIGHEST)

    outer_mix = jnp.einsum(
        "kmi,ikc->mkc", second_factor, columns, preferred_element_type=jnp.float32
    ).astype(jnp.bfloat16)
    d_inner = jnp.einsum(
        "kmi,mkc->ikc", second_factor, d_outer, preferred_element_type=jnp.float32
    ).astype(jnp.bfloat16)
    d_second_part = jnp.einsum(
        "mkc,ikc->kmi", d_outer, columns, preferred_element_type=jnp.float32
    )

    outer_send = outer_mix.reshape(n_seq, blocks_here, k_here, chan_rows)
    dinner_send = d_inner.reshape(n_seq, blocks_here, k_here, chan_rows)
    piece = jnp.concatenate(
        [
            pooled_here.reshape(n_a),
            per_doc_here.reshape(n_b),
            xdoc_here.reshape(n_b),
            g_part.reshape(n_a),
        ]
    )
    piece_b = jnp.broadcast_to(split_hi_lo(piece)[None, :], (n_seq, 2 * piece.shape[0]))
    send3 = jnp.concatenate(
        [jnp.concatenate([outer_send, dinner_send], axis=3).reshape(n_seq, -1), piece_b], axis=1
    )
    recv3_all = seq_exchange(send3)
    recv3 = recv3_all[:, :n_mix].reshape(n_seq, blocks_here, k_here, 2 * chan_rows)
    gath3 = join_hi_lo(recv3_all[:, n_mix:])
    outer_tok = (
        recv3[..., :chan_rows].transpose(3, 1, 0, 2).reshape(chan_rows, tok_cols).astype(jnp.float32)
    )
    d_rows = recv3[..., chan_rows:].transpose(1, 0, 2, 3).reshape(
        blocks_here, n_seq * k_here, chan_rows
    )
    pooled = gath3[:, :n_a].reshape(n_doc, lat)
    per_doc = (
        gath3[:, n_a : n_a + n_b].reshape(n_seq, chan_rows, docs_here).transpose(1, 0, 2)
    ).reshape(chan_rows, n_doc)
    xdoc = (
        gath3[:, n_a + n_b : n_a + 2 * n_b].reshape(n_seq, chan_rows, docs_here).transpose(1, 0, 2)
    ).reshape(chan_rows, n_doc)
    g_gath = gath3[:, n_a + 2 * n_b :].reshape(1, n_doc * lat)

    spread = jnp.einsum("dl,cl->cd", pooled, up_float, precision=HIGHEST)
    summary = jnp.dot(spread, member, precision=HIGHEST)
    mixed = outer_tok + summary
    hidden = (act * mixed).astype(jnp.bfloat16)
    d_gate_bf = (upstream * mixed * sig * (1.0 + gate_pre * (1.0 - sig))).astype(jnp.bfloat16)

    d_value_bf = (
        jnp.einsum("ikj,ikc->cij", first_factor, d_rows, preferred_element_type=jnp.float32)
        .astype(jnp.bfloat16)
        .reshape(chan_rows, tok_cols)
    )
    d_first_part = jnp.einsum("ikc,cij->ikj", d_rows, blocked, preferred_element_type=jnp.float32)
    d_up = jnp.einsum("cd,dl->cl", per_doc, pooled, precision=HIGHEST)

    both_grads = jnp.concatenate([d_gate_bf, d_value_bf], axis=0)
    d_proj_part = jnp.einsum("ot,it->oi", both_grads, gathered, preferred_element_type=jnp.float32)
    rows_here = 2 * chan_rows // n_seq
    width = d_proj_part.shape[1]

    proj_send = d_proj_part.reshape(n_seq, rows_here, width).astype(jnp.bfloat16)
    proj_red = jnp.sum(seq_exchange(proj_send).astype(jnp.float32), axis=0)
    k_part = block_width // n_chan
    m_part = n_blk2 // n_chan
    first_send = (
        d_first_part.reshape(blocks_here, n_chan, k_part, block_width)
        .transpose(1, 0, 2, 3)
        .reshape(n_chan, -1)
    )
    second_send = (
        d_second_part.reshape(k_here, n_chan, m_part, n_blk2).transpose(1, 0, 2, 3).reshape(n_chan, -1)
    )
    g_send = jnp.broadcast_to(g_gath, (n_chan, n_doc * lat))
    fac_send = jnp.concatenate([first_send, second_send, g_send], axis=1)
    fac_red = lax.psum_scatter(fac_send.reshape(-1, 128), "chan", scatter_dimension=0, tiled=True)
    fac_red = fac_red.reshape(-1)
    n_f = blocks_here * k_part * block_width
    d_first = fac_red[:n_f].reshape(blocks_here, k_part, block_width)
    n_s = k_here * m_part * n_blk2
    d_second = fac_red[n_f : n_f + n_s].reshape(k_here, m_part, n_blk2)
    g_full = fac_red[n_f + n_s :].reshape(n_doc, lat)

    proj_bf = proj_red.astype(jnp.bfloat16)
    gath5 = seq_exchange(jnp.broadcast_to(proj_bf[None], (n_seq, rows_here, width)))
    d_proj = gath5.reshape(2 * chan_rows, width).astype(jnp.float32)
    d_pooled = g_full * len_scale[:, None]
    d_down = jnp.einsum(
        "cd,dl->cl", xdoc, d_pooled.astype(jnp.bfloat16).astype(jnp.float32), precision=HIGHEST
    )
    return (hidden, d_proj[:chan_rows], d_proj[chan_rows:], d_first, d_second, d_down, d_up)


def solution(mesh):
    in_specs = (
        P("chan", "seq"),
        P("chan", None),
        P("chan", None),
        P("seq", None, None),
        P("seq", None, None),
        P("chan", None),
        P("chan", None),
        P(),
        P("chan", "seq"),
    )
    out_specs = (
        P("chan", "seq"),
        P("chan", None),
        P("chan", None),
        P("seq", "chan", None),
        P("seq", "chan", None),
        P("chan", None),
        P("chan", None),
    )

    return jax.shard_map(body, mesh=mesh, in_specs=in_specs, out_specs=out_specs, check_vma=False)
```

```python
import jax
import jax.numpy as jnp
from jax import lax
from jax.sharding import PartitionSpec as P


HIGHEST = lax.Precision.HIGHEST


def seq_exchange(x):
    return lax.all_to_all(x, "seq", 0, 0, tiled=True)


def split_hi_lo(x):
    hi = lax.reduce_precision(x, exponent_bits=8, mantissa_bits=7)
    lo = x - hi
    return jnp.concatenate([hi.astype(jnp.bfloat16), lo.astype(jnp.bfloat16)], axis=-1)


def join_hi_lo(x):
    n = x.shape[-1] // 2
    return x[..., :n].astype(jnp.float32) + x[..., n:].astype(jnp.float32)


def body(
    tokens,
    gate_weight,
    value_weight,
    first_factor,
    second_factor,
    down_latent,
    up_latent,
    doc_lengths,
    cotangent,
):
    n_seq = lax.axis_size("seq")
    n_chan = lax.axis_size("chan")
    chan_rows, tok_cols = tokens.shape
    blocks_here, block_width, _ = first_factor.shape
    k_here, n_blk2, _ = second_factor.shape
    lat = down_latent.shape[1]
    n_doc = doc_lengths.shape[0]
    docs_here = n_doc // n_seq
    me = lax.axis_index("seq")

    packed = jnp.concatenate([tokens, down_latent], axis=1)
    gathered_all = lax.all_gather(packed, "chan", axis=0, tiled=True)
    gathered = gathered_all[:, :tok_cols]
    down_full = gathered_all[:, tok_cols:]

    doc_ends = jnp.cumsum(doc_lengths)
    doc_begins = doc_ends - doc_lengths
    position = me * tok_cols + jnp.arange(tok_cols, dtype=jnp.int32)
    member = (
        (position[None, :] >= doc_begins[:, None]) & (position[None, :] < doc_ends[:, None])
    ).astype(jnp.float32)
    len_scale = lax.rsqrt(doc_lengths.astype(jnp.float32))

    gate_pre = jnp.dot(gate_weight, gathered, preferred_element_type=jnp.float32)
    value_bf = jnp.dot(value_weight, gathered, preferred_element_type=jnp.float32).astype(
        jnp.bfloat16
    )
    latent = jnp.einsum("ct,cl->lt", gathered, down_full, preferred_element_type=jnp.float32)
    doc_lat_part = jnp.einsum("dt,lt->dl", member, latent, precision=HIGHEST)
    xdoc_part = jnp.einsum(
        "ct,dt->cd", tokens, member.astype(jnp.bfloat16), preferred_element_type=jnp.float32
    )

    blocked = value_bf.reshape(chan_rows, blocks_here, block_width)
    inner_mix = jnp.einsum(
        "ikj,cij->ikc", first_factor, blocked, preferred_element_type=jnp.float32
    ).astype(jnp.bfloat16)

    sig = jax.nn.sigmoid(gate_pre)
    act = gate_pre * sig
    upstream = cotangent.astype(jnp.float32)
    d_mixed = upstream * act
    d_mixed_bf = d_mixed.astype(jnp.bfloat16)
    per_doc_part = jnp.einsum("ct,dt->cd", d_mixed, member, precision=HIGHEST)

    inner_send = inner_mix.reshape(blocks_here, n_seq, k_here, chan_rows).transpose(1, 0, 2, 3)
    d_send = d_mixed_bf.reshape(chan_rows, blocks_here, n_seq, k_here).transpose(2, 1, 3, 0)
    mix_send = jnp.concatenate([inner_send, d_send], axis=3).reshape(n_seq, -1)
    n_mix = mix_send.shape[1]

    small_send = jnp.concatenate(
        [
            doc_lat_part.reshape(n_seq, docs_here * lat),
            per_doc_part.reshape(chan_rows, n_seq, docs_here)
            .transpose(1, 0, 2)
            .reshape(n_seq, chan_rows * docs_here),
            xdoc_part.reshape(chan_rows, n_seq, docs_here)
            .transpose(1, 0, 2)
            .reshape(n_seq, chan_rows * docs_here),
        ],
        axis=1,
    )
    recv2 = seq_exchange(jnp.concatenate([mix_send, split_hi_lo(small_send)], axis=1))
    mix2 = recv2[:, :n_mix].reshape(n_seq, blocks_here, k_here, 2 * chan_rows)
    columns = mix2[..., :chan_rows].reshape(n_seq * blocks_here, k_here, chan_rows)
    d_outer = mix2[..., chan_rows:].reshape(n_seq * blocks_here, k_here, chan_rows)
    small_red = jnp.sum(join_hi_lo(recv2[:, n_mix:]), axis=0)
    n_a = docs_here * lat
    n_b = chan_rows * docs_here
    scale_here = lax.dynamic_slice(len_scale, (me * docs_here,), (docs_here,))
    pooled_here = small_red[:n_a].reshape(docs_here, lat) * scale_here[:, None]
    per_doc_here = small_red[n_a : n_a + n_b].reshape(chan_rows, docs_here)
    xdoc_here = small_red[n_a + n_b :].reshape(chan_rows, docs_here)

    up_float = up_latent.astype(jnp.float32)
    g_part = jnp.einsum("cd,cl->dl", per_doc_here, up_float, precision=HIGHEST)

    outer_mix = jnp.einsum(
        "kmi,ikc->mkc", second_factor, columns, preferred_element_type=jnp.float32
    ).astype(jnp.bfloat16)
    d_inner = jnp.einsum(
        "kmi,mkc->ikc", second_factor, d_outer, preferred_element_type=jnp.float32
    ).astype(jnp.bfloat16)
    d_second_part = jnp.einsum(
        "mkc,ikc->kmi", d_outer, columns, preferred_element_type=jnp.float32
    )

    outer_send = outer_mix.reshape(n_seq, blocks_here, k_here, chan_rows)
    dinner_send = d_inner.reshape(n_seq, blocks_here, k_here, chan_rows)
    piece = jnp.concatenate(
        [
            pooled_here.reshape(n_a),
            per_doc_here.reshape(n_b),
            xdoc_here.reshape(n_b),
            g_part.reshape(n_a),
        ]
    )
    piece_b = jnp.broadcast_to(split_hi_lo(piece)[None, :], (n_seq, 2 * piece.shape[0]))
    send3 = jnp.concatenate(
        [jnp.concatenate([outer_send, dinner_send], axis=3).reshape(n_seq, -1), piece_b], axis=1
    )
    recv3_all = seq_exchange(send3)
    recv3 = recv3_all[:, :n_mix].reshape(n_seq, blocks_here, k_here, 2 * chan_rows)
    gath3 = join_hi_lo(recv3_all[:, n_mix:])
    outer_tok = (
        recv3[..., :chan_rows].transpose(3, 1, 0, 2).reshape(chan_rows, tok_cols).astype(jnp.float32)
    )
    d_rows = recv3[..., chan_rows:].transpose(1, 0, 2, 3).reshape(
        blocks_here, n_seq * k_here, chan_rows
    )
    pooled = gath3[:, :n_a].reshape(n_doc, lat)
    per_doc = (
        gath3[:, n_a : n_a + n_b].reshape(n_seq, chan_rows, docs_here).transpose(1, 0, 2)
    ).reshape(chan_rows, n_doc)
    xdoc = (
        gath3[:, n_a + n_b : n_a + 2 * n_b].reshape(n_seq, chan_rows, docs_here).transpose(1, 0, 2)
    ).reshape(chan_rows, n_doc)
    g_gath = gath3[:, n_a + 2 * n_b :].reshape(1, n_doc * lat)

    spread = jnp.einsum("dl,cl->cd", pooled, up_float, precision=HIGHEST)
    summary = jnp.dot(spread, member, precision=HIGHEST)
    mixed = outer_tok + summary
    hidden = (act * mixed).astype(jnp.bfloat16)
    d_gate_bf = (upstream * mixed * sig * (1.0 + gate_pre * (1.0 - sig))).astype(jnp.bfloat16)

    d_value_bf = (
        jnp.einsum("ikj,ikc->cij", first_factor, d_rows, preferred_element_type=jnp.float32)
        .astype(jnp.bfloat16)
        .reshape(chan_rows, tok_cols)
    )
    d_first_part = jnp.einsum("ikc,cij->ikj", d_rows, blocked, preferred_element_type=jnp.float32)
    d_up = jnp.einsum("cd,dl->cl", per_doc, pooled, precision=HIGHEST)

    both_grads = jnp.concatenate([d_gate_bf, d_value_bf], axis=0)
    d_proj_part = jnp.einsum("ot,it->oi", both_grads, gathered, preferred_element_type=jnp.float32)
    rows_here = 2 * chan_rows // n_seq
    width = d_proj_part.shape[1]

    proj_send = d_proj_part.reshape(n_seq, rows_here, width).astype(jnp.bfloat16)
    proj_red = jnp.sum(seq_exchange(proj_send).astype(jnp.float32), axis=0)
    k_part = block_width // n_chan
    m_part = n_blk2 // n_chan
    first_send = (
        d_first_part.reshape(blocks_here, n_chan, k_part, block_width)
        .transpose(1, 0, 2, 3)
        .reshape(n_chan, -1)
    )
    second_send = (
        d_second_part.reshape(k_here, n_chan, m_part, n_blk2).transpose(1, 0, 2, 3).reshape(n_chan, -1)
    )
    g_send = jnp.broadcast_to(g_gath, (n_chan, n_doc * lat))
    fac_send = jnp.concatenate([first_send, second_send, g_send], axis=1)
    fac_red = lax.psum_scatter(fac_send.reshape(-1, 128), "chan", scatter_dimension=0, tiled=True)
    proj_bf = proj_red.astype(jnp.bfloat16)
    gath5 = seq_exchange(jnp.broadcast_to(proj_bf[None], (n_seq, rows_here, width)))
    fac_red = fac_red.reshape(-1)
    n_f = blocks_here * k_part * block_width
    d_first = fac_red[:n_f].reshape(blocks_here, k_part, block_width)
    n_s = k_here * m_part * n_blk2
    d_second = fac_red[n_f : n_f + n_s].reshape(k_here, m_part, n_blk2)
    g_full = fac_red[n_f + n_s :].reshape(n_doc, lat)
    d_pooled = lax.reduce_precision(g_full * len_scale[:, None], exponent_bits=8, mantissa_bits=7)
    d_down = jnp.einsum("cd,dl->cl", xdoc, d_pooled, precision=HIGHEST)
    d_proj = gath5.reshape(2 * chan_rows, width).astype(jnp.float32)
    return (hidden, d_proj[:chan_rows], d_proj[chan_rows:], d_first, d_second, d_down, d_up)


def solution(mesh):
    in_specs = (
        P("chan", "seq"),
        P("chan", None),
        P("chan", None),
        P("seq", None, None),
        P("seq", None, None),
        P("chan", None),
        P("chan", None),
        P(),
        P("chan", "seq"),
    )
    out_specs = (
        P("chan", "seq"),
        P("chan", None),
        P("chan", None),
        P("seq", "chan", None),
        P("seq", "chan", None),
        P("chan", None),
        P("chan", None),
    )

    return jax.shard_map(body, mesh=mesh, in_specs=in_specs, out_specs=out_specs, check_vma=False)
```

```python
import jax
import jax.numpy as jnp
from jax import lax
from jax.sharding import PartitionSpec as P
from jax.experimental import pallas as pl
from jax.experimental.pallas import tpu as pltpu


HIGHEST = lax.Precision.HIGHEST


def seq_exchange(x):
    return lax.all_to_all(x, "seq", 0, 0, tiled=True)


def tiled_exchange(x):
    n, width = x.shape
    unit = 8 * 128
    padded = -(-width // unit) * unit
    x = jnp.pad(x, ((0, 0), (0, padded - width))).reshape(n, padded // 128, 128)
    return seq_exchange(x).reshape(n, padded)[:, :width]


def split_hi_lo(x):
    hi = lax.reduce_precision(x, exponent_bits=8, mantissa_bits=7)
    lo = x - hi
    return jnp.concatenate([hi.astype(jnp.bfloat16), lo.astype(jnp.bfloat16)], axis=-1)


def join_hi_lo(x):
    n = x.shape[-1] // 2
    return x[..., :n].astype(jnp.float32) + x[..., n:].astype(jnp.float32)


def epilogue_kernel(fac_ref, xdoc_ref, scale_ref, first_ref, second_ref, down_ref):
    blocks, kp, width = first_ref.shape
    k_here, m_part, nb2 = second_ref.shape
    lanes = fac_ref.shape[1]
    rows_first = blocks * kp * width // lanes
    per_row = width // lanes
    for i in range(blocks):
        for h in range(per_row):
            first_ref[i, :, pl.ds(h * lanes, lanes)] = fac_ref[pl.ds(i * kp * per_row + h, kp, stride=per_row), :]
    rows_second = k_here * m_part * nb2 // lanes
    per_lane_row = lanes // nb2
    for k in range(k_here):
        for m in range(m_part):
            r = rows_first + (k * m_part + m) // per_lane_row
            off = (m % per_lane_row) * nb2
            second_ref[k, pl.ds(m, 1), :] = fac_ref[pl.ds(r, 1), pl.ds(off, nb2)]
    g0 = rows_first + rows_second
    g = fac_ref[pl.ds(g0, fac_ref.shape[0] - g0), :]
    dp = lax.reduce_precision(g * scale_ref[...], exponent_bits=8, mantissa_bits=7)
    down_ref[...] = jnp.dot(xdoc_ref[...], dp, precision=HIGHEST, preferred_element_type=jnp.float32)


def epilogue(fac, xdoc, scale_col, first_shape, second_shape):
    f32 = jnp.float32
    vmem = pl.BlockSpec(memory_space=pltpu.VMEM)
    return pl.pallas_call(
        epilogue_kernel,
        out_shape=(jax.ShapeDtypeStruct(first_shape, f32), jax.ShapeDtypeStruct(second_shape, f32),
                   jax.ShapeDtypeStruct((xdoc.shape[0], fac.shape[1]), f32)),
        in_specs=[vmem] * 3,
        out_specs=[vmem] * 3,
        cost_estimate=pl.CostEstimate(
            flops=2 * xdoc.shape[0] * xdoc.shape[1] * fac.shape[1] * 6,
            bytes_accessed=4 * (2 * fac.size + xdoc.size + xdoc.shape[0] * fac.shape[1]),
            transcendentals=0,
        ),
    )(fac, xdoc, scale_col)


def body(
    tokens,
    gate_weight,
    value_weight,
    first_factor,
    second_factor,
    down_latent,
    up_latent,
    doc_lengths,
    cotangent,
):
    n_seq = lax.axis_size("seq")
    n_chan = lax.axis_size("chan")
    chan_rows, tok_cols = tokens.shape
    blocks_here, block_width, _ = first_factor.shape
    k_here, n_blk2, _ = second_factor.shape
    lat = down_latent.shape[1]
    n_doc = doc_lengths.shape[0]
    docs_here = n_doc // n_seq
    me = lax.axis_index("seq")

    packed = jnp.concatenate([tokens, down_latent], axis=1)
    gathered_all = lax.all_gather(packed, "chan", axis=0, tiled=True)
    gathered = gathered_all[:, :tok_cols]
    down_full = gathered_all[:, tok_cols:]

    doc_ends = jnp.cumsum(doc_lengths)
    doc_begins = doc_ends - doc_lengths
    position = me * tok_cols + jnp.arange(tok_cols, dtype=jnp.int32)
    member = (
        (position[None, :] >= doc_begins[:, None]) & (position[None, :] < doc_ends[:, None])
    ).astype(jnp.float32)
    len_scale = lax.rsqrt(doc_lengths.astype(jnp.float32))

    gate_pre = jnp.dot(gate_weight, gathered, preferred_element_type=jnp.float32)
    value_bf = jnp.dot(value_weight, gathered, preferred_element_type=jnp.float32).astype(
        jnp.bfloat16
    )
    latent = jnp.einsum("ct,cl->lt", gathered, down_full, preferred_element_type=jnp.float32)
    doc_lat_part = jnp.einsum("dt,lt->dl", member, latent, precision=HIGHEST)
    xdoc_part = jnp.einsum(
        "ct,dt->cd", tokens, member.astype(jnp.bfloat16), preferred_element_type=jnp.float32
    )

    blocked = value_bf.reshape(chan_rows, blocks_here, block_width)
    inner_mix = jnp.einsum(
        "ikj,cij->ikc", first_factor, blocked, preferred_element_type=jnp.float32
    ).astype(jnp.bfloat16)

    sig = jax.nn.sigmoid(gate_pre)
    act = gate_pre * sig
    upstream = cotangent.astype(jnp.float32)
    d_mixed = upstream * act
    d_mixed_bf = d_mixed.astype(jnp.bfloat16)
    per_doc_part = jnp.einsum("ct,dt->cd", d_mixed, member, precision=HIGHEST)

    inner_send = inner_mix.reshape(blocks_here, n_seq, k_here, chan_rows).transpose(1, 0, 2, 3)
    d_send = d_mixed_bf.reshape(chan_rows, blocks_here, n_seq, k_here).transpose(2, 1, 3, 0)
    mix_send = jnp.concatenate([inner_send, d_send], axis=3).reshape(n_seq, -1)
    n_mix = mix_send.shape[1]

    small_send = jnp.concatenate(
        [
            doc_lat_part.reshape(n_seq, docs_here * lat),
            per_doc_part.reshape(chan_rows, n_seq, docs_here)
            .transpose(1, 0, 2)
            .reshape(n_seq, chan_rows * docs_here),
            xdoc_part.reshape(chan_rows, n_seq, docs_here)
            .transpose(1, 0, 2)
            .reshape(n_seq, chan_rows * docs_here),
        ],
        axis=1,
    )
    recv2 = tiled_exchange(jnp.concatenate([mix_send, split_hi_lo(small_send)], axis=1))
    mix2 = recv2[:, :n_mix].reshape(n_seq, blocks_here, k_here, 2 * chan_rows)
    columns = mix2[..., :chan_rows].reshape(n_seq * blocks_here, k_here, chan_rows)
    d_outer = mix2[..., chan_rows:].reshape(n_seq * blocks_here, k_here, chan_rows)
    small_red = jnp.sum(join_hi_lo(recv2[:, n_mix:]), axis=0)
    n_a = docs_here * lat
    n_b = chan_rows * docs_here
    scale_here = lax.dynamic_slice(len_scale, (me * docs_here,), (docs_here,))
    pooled_here = small_red[:n_a].reshape(docs_here, lat) * scale_here[:, None]
    per_doc_here = small_red[n_a : n_a + n_b].reshape(chan_rows, docs_here)
    xdoc_here = small_red[n_a + n_b :].reshape(chan_rows, docs_here)

    up_float = up_latent.astype(jnp.float32)
    g_part = jnp.einsum("cd,cl->dl", per_doc_here, up_float, precision=HIGHEST)

    outer_mix = jnp.einsum(
        "kmi,ikc->mkc", second_factor, columns, preferred_element_type=jnp.float32
    ).astype(jnp.bfloat16)
    d_inner = jnp.einsum(
        "kmi,mkc->ikc", second_factor, d_outer, preferred_element_type=jnp.float32
    ).astype(jnp.bfloat16)
    d_second_part = jnp.einsum(
        "mkc,ikc->kmi", d_outer, columns, preferred_element_type=jnp.float32
    )

    outer_send = outer_mix.reshape(n_seq, blocks_here, k_here, chan_rows)
    dinner_send = d_inner.reshape(n_seq, blocks_here, k_here, chan_rows)
    piece = jnp.concatenate(
        [
            pooled_here.reshape(n_a),
            per_doc_here.reshape(n_b),
            xdoc_here.reshape(n_b),
            g_part.reshape(n_a),
        ]
    )
    piece_b = jnp.broadcast_to(split_hi_lo(piece)[None, :], (n_seq, 2 * piece.shape[0]))
    send3 = jnp.concatenate(
        [jnp.concatenate([outer_send, dinner_send], axis=3).reshape(n_seq, -1), piece_b], axis=1
    )
    recv3_all = tiled_exchange(send3)
    recv3 = recv3_all[:, :n_mix].reshape(n_seq, blocks_here, k_here, 2 * chan_rows)
    gath3 = join_hi_lo(recv3_all[:, n_mix:])
    outer_tok = (
        recv3[..., :chan_rows].transpose(3, 1, 0, 2).reshape(chan_rows, tok_cols).astype(jnp.float32)
    )
    d_rows = recv3[..., chan_rows:].transpose(1, 0, 2, 3).reshape(
        blocks_here, n_seq * k_here, chan_rows
    )
    pooled = gath3[:, :n_a].reshape(n_doc, lat)
    per_doc = (
        gath3[:, n_a : n_a + n_b].reshape(n_seq, chan_rows, docs_here).transpose(1, 0, 2)
    ).reshape(chan_rows, n_doc)
    xdoc = (
        gath3[:, n_a + n_b : n_a + 2 * n_b].reshape(n_seq, chan_rows, docs_here).transpose(1, 0, 2)
    ).reshape(chan_rows, n_doc)
    g_gath = gath3[:, n_a + 2 * n_b :].reshape(1, n_doc * lat)

    spread = jnp.einsum("dl,cl->cd", pooled, up_float, precision=HIGHEST)
    summary = jnp.dot(spread, member, precision=HIGHEST)
    mixed = outer_tok + summary
    hidden = (act * mixed).astype(jnp.bfloat16)
    d_gate_bf = (upstream * mixed * sig * (1.0 + gate_pre * (1.0 - sig))).astype(jnp.bfloat16)

    d_value_bf = (
        jnp.einsum("ikj,ikc->cij", first_factor, d_rows, preferred_element_type=jnp.float32)
        .astype(jnp.bfloat16)
        .reshape(chan_rows, tok_cols)
    )
    d_first_part = jnp.einsum("ikc,cij->ikj", d_rows, blocked, preferred_element_type=jnp.float32)
    d_up = jnp.einsum("cd,dl->cl", per_doc, pooled, precision=HIGHEST)

    both_grads = jnp.concatenate([d_gate_bf, d_value_bf], axis=0)
    d_proj_part = jnp.einsum("ot,it->oi", both_grads, gathered, preferred_element_type=jnp.float32)
    rows_here = 2 * chan_rows // n_seq
    width = d_proj_part.shape[1]

    proj_send = d_proj_part.reshape(n_seq, rows_here, width).astype(jnp.bfloat16)
    proj_red = jnp.sum(seq_exchange(proj_send).astype(jnp.float32), axis=0)
    k_part = block_width // n_chan
    m_part = n_blk2 // n_chan
    first_send = (
        d_first_part.reshape(blocks_here, n_chan, k_part, block_width)
        .transpose(1, 0, 2, 3)
        .reshape(n_chan, -1)
    )
    second_send = (
        d_second_part.reshape(k_here, n_chan, m_part, n_blk2).transpose(1, 0, 2, 3).reshape(n_chan, -1)
    )
    g_send = jnp.broadcast_to(g_gath, (n_chan, n_doc * lat))
    fac_send = jnp.concatenate([first_send, second_send, g_send], axis=1)
    fac_red = lax.psum_scatter(fac_send.reshape(-1, 128), "chan", scatter_dimension=0, tiled=True)
    proj_bf = proj_red.astype(jnp.bfloat16)
    gath5 = seq_exchange(jnp.broadcast_to(proj_bf[None], (n_seq, rows_here, width)))
    d_first, d_second, d_down = epilogue(
        fac_red,
        xdoc,
        len_scale.reshape(n_doc, 1),
        (blocks_here, k_part, block_width),
        (k_here, m_part, n_blk2),
    )
    d_proj = gath5.reshape(2 * chan_rows, width).astype(jnp.float32)
    return (hidden, d_proj[:chan_rows], d_proj[chan_rows:], d_first, d_second, d_down, d_up)


def solution(mesh):
    in_specs = (
        P("chan", "seq"),
        P("chan", None),
        P("chan", None),
        P("seq", None, None),
        P("seq", None, None),
        P("chan", None),
        P("chan", None),
        P(),
        P("chan", "seq"),
    )
    out_specs = (
        P("chan", "seq"),
        P("chan", None),
        P("chan", None),
        P("seq", "chan", None),
        P("seq", "chan", None),
        P("chan", None),
        P("chan", None),
    )

    return jax.shard_map(body, mesh=mesh, in_specs=in_specs, out_specs=out_specs, check_vma=False)
```

```python
import jax
import jax.numpy as jnp
from jax import lax
from jax.sharding import PartitionSpec as P
from jax.experimental import pallas as pl
from jax.experimental.pallas import tpu as pltpu


HIGHEST = lax.Precision.HIGHEST


def seq_exchange(x):
    return lax.all_to_all(x, "seq", 0, 0, tiled=True)


def split_hi_lo(x):
    hi = lax.reduce_precision(x, exponent_bits=8, mantissa_bits=7)
    lo = x - hi
    return jnp.concatenate([hi.astype(jnp.bfloat16), lo.astype(jnp.bfloat16)], axis=-1)


def join_hi_lo(x):
    n = x.shape[-1] // 2
    return x[..., :n].astype(jnp.float32) + x[..., n:].astype(jnp.float32)


def epilogue_kernel(fac_ref, xdoc_ref, scale_ref, first_ref, second_ref, down_ref):
    blocks, kp, width = first_ref.shape
    k_here, m_part, nb2 = second_ref.shape
    lanes = fac_ref.shape[1]
    rows_first = blocks * kp * width // lanes
    per_row = width // lanes
    for i in range(blocks):
        for h in range(per_row):
            first_ref[i, :, pl.ds(h * lanes, lanes)] = fac_ref[pl.ds(i * kp * per_row + h, kp, stride=per_row), :]
    rows_second = k_here * m_part * nb2 // lanes
    per_lane_row = lanes // nb2
    for k in range(k_here):
        for m in range(m_part):
            r = rows_first + (k * m_part + m) // per_lane_row
            off = (m % per_lane_row) * nb2
            second_ref[k, pl.ds(m, 1), :] = fac_ref[pl.ds(r, 1), pl.ds(off, nb2)]
    g0 = rows_first + rows_second
    g = fac_ref[pl.ds(g0, fac_ref.shape[0] - g0), :]
    dp = lax.reduce_precision(g * scale_ref[...], exponent_bits=8, mantissa_bits=7)
    down_ref[...] = jnp.dot(xdoc_ref[...], dp, precision=HIGHEST, preferred_element_type=jnp.float32)


def epilogue(fac, xdoc, scale_col, first_shape, second_shape):
    f32 = jnp.float32
    vmem = pl.BlockSpec(memory_space=pltpu.VMEM)
    return pl.pallas_call(
        epilogue_kernel,
        out_shape=(jax.ShapeDtypeStruct(first_shape, f32), jax.ShapeDtypeStruct(second_shape, f32),
                   jax.ShapeDtypeStruct((xdoc.shape[0], fac.shape[1]), f32)),
        in_specs=[vmem] * 3,
        out_specs=[vmem] * 3,
        cost_estimate=pl.CostEstimate(
            flops=2 * xdoc.shape[0] * xdoc.shape[1] * fac.shape[1] * 6,
            bytes_accessed=4 * (2 * fac.size + xdoc.size + xdoc.shape[0] * fac.shape[1]),
            transcendentals=0,
        ),
    )(fac, xdoc, scale_col)


def proj_kernel(in_ref, gate_ref, val_ref):
    n, rows, _ = in_ref.shape
    half = n // 2
    for s in range(n):
        dst = gate_ref if s < half else val_ref
        dst[pl.ds((s % half) * rows, rows), :] = in_ref[s].astype(jnp.float32)


def proj_unpack(gath):
    n, rows, width = gath.shape
    shape = jax.ShapeDtypeStruct((n // 2 * rows, width), jnp.float32)
    vmem = pl.BlockSpec(memory_space=pltpu.VMEM)
    return pl.pallas_call(
        proj_kernel,
        out_shape=(shape, shape),
        in_specs=[vmem],
        out_specs=[vmem, vmem],
        cost_estimate=pl.CostEstimate(flops=0, bytes_accessed=gath.size * 6, transcendentals=0),
    )(gath)


def body(
    tokens,
    gate_weight,
    value_weight,
    first_factor,
    second_factor,
    down_latent,
    up_latent,
    doc_lengths,
    cotangent,
):
    n_seq = lax.axis_size("seq")
    n_chan = lax.axis_size("chan")
    chan_rows, tok_cols = tokens.shape
    blocks_here, block_width, _ = first_factor.shape
    k_here, n_blk2, _ = second_factor.shape
    lat = down_latent.shape[1]
    n_doc = doc_lengths.shape[0]
    docs_here = n_doc // n_seq
    me = lax.axis_index("seq")

    packed = jnp.concatenate([tokens, down_latent], axis=1)
    gathered_all = lax.all_gather(packed, "chan", axis=0, tiled=True)
    gathered = gathered_all[:, :tok_cols]
    down_full = gathered_all[:, tok_cols:]

    doc_ends = jnp.cumsum(doc_lengths)
    doc_begins = doc_ends - doc_lengths
    position = me * tok_cols + jnp.arange(tok_cols, dtype=jnp.int32)
    member = (
        (position[None, :] >= doc_begins[:, None]) & (position[None, :] < doc_ends[:, None])
    ).astype(jnp.float32)
    len_scale = lax.rsqrt(doc_lengths.astype(jnp.float32))

    gate_pre = jnp.dot(gate_weight, gathered, preferred_element_type=jnp.float32)
    value_bf = jnp.dot(value_weight, gathered, preferred_element_type=jnp.float32).astype(
        jnp.bfloat16
    )
    latent = jnp.einsum("ct,cl->lt", gathered, down_full, preferred_element_type=jnp.float32)
    doc_lat_part = jnp.einsum("dt,lt->dl", member, latent, precision=HIGHEST)
    xdoc_part = jnp.einsum(
        "ct,dt->cd", tokens, member.astype(jnp.bfloat16), preferred_element_type=jnp.float32
    )

    blocked = value_bf.reshape(chan_rows, blocks_here, block_width)
    inner_mix = jnp.einsum(
        "ikj,cij->ikc", first_factor, blocked, preferred_element_type=jnp.float32
    ).astype(jnp.bfloat16)

    sig = jax.nn.sigmoid(gate_pre)
    act = gate_pre * sig
    upstream = cotangent.astype(jnp.float32)
    d_mixed = upstream * act
    d_mixed_bf = d_mixed.astype(jnp.bfloat16)
    per_doc_part = jnp.einsum("ct,dt->cd", d_mixed, member, precision=HIGHEST)

    inner_send = inner_mix.reshape(blocks_here, n_seq, k_here, chan_rows).transpose(1, 0, 2, 3)
    d_send = d_mixed_bf.reshape(chan_rows, blocks_here, n_seq, k_here).transpose(2, 1, 3, 0)
    mix_send = jnp.concatenate([inner_send, d_send], axis=3).reshape(n_seq, -1)
    n_mix = mix_send.shape[1]

    small_send = jnp.concatenate(
        [
            doc_lat_part.reshape(n_seq, docs_here * lat),
            per_doc_part.reshape(chan_rows, n_seq, docs_here)
            .transpose(1, 0, 2)
            .reshape(n_seq, chan_rows * docs_here),
            xdoc_part.reshape(chan_rows, n_seq, docs_here)
            .transpose(1, 0, 2)
            .reshape(n_seq, chan_rows * docs_here),
        ],
        axis=1,
    )
    recv2 = seq_exchange(jnp.concatenate([mix_send, split_hi_lo(small_send)], axis=1))
    mix2 = recv2[:, :n_mix].reshape(n_seq, blocks_here, k_here, 2 * chan_rows)
    columns = mix2[..., :chan_rows].reshape(n_seq * blocks_here, k_here, chan_rows)
    d_outer = mix2[..., chan_rows:].reshape(n_seq * blocks_here, k_here, chan_rows)
    small_red = jnp.sum(join_hi_lo(recv2[:, n_mix:]), axis=0)
    n_a = docs_here * lat
    n_b = chan_rows * docs_here
    scale_here = lax.dynamic_slice(len_scale, (me * docs_here,), (docs_here,))
    pooled_here = small_red[:n_a].reshape(docs_here, lat) * scale_here[:, None]
    per_doc_here = small_red[n_a : n_a + n_b].reshape(chan_rows, docs_here)
    xdoc_here = small_red[n_a + n_b :].reshape(chan_rows, docs_here)

    up_float = up_latent.astype(jnp.float32)
    g_part = jnp.einsum("cd,cl->dl", per_doc_here, up_float, precision=HIGHEST)

    outer_mix = jnp.einsum(
        "kmi,ikc->mkc", second_factor, columns, preferred_element_type=jnp.float32
    ).astype(jnp.bfloat16)
    d_inner = jnp.einsum(
        "kmi,mkc->ikc", second_factor, d_outer, preferred_element_type=jnp.float32
    ).astype(jnp.bfloat16)
    d_second_part = jnp.einsum(
        "mkc,ikc->kmi", d_outer, columns, preferred_element_type=jnp.float32
    )

    outer_send = outer_mix.reshape(n_seq, blocks_here, k_here, chan_rows)
    dinner_send = d_inner.reshape(n_seq, blocks_here, k_here, chan_rows)
    piece = jnp.concatenate(
        [
            pooled_here.reshape(n_a),
            per_doc_here.reshape(n_b),
            xdoc_here.reshape(n_b),
            g_part.reshape(n_a),
        ]
    )
    piece_b = jnp.broadcast_to(split_hi_lo(piece)[None, :], (n_seq, 2 * piece.shape[0]))
    send3 = jnp.concatenate(
        [jnp.concatenate([outer_send, dinner_send], axis=3).reshape(n_seq, -1), piece_b], axis=1
    )
    recv3_all = seq_exchange(send3)
    recv3 = recv3_all[:, :n_mix].reshape(n_seq, blocks_here, k_here, 2 * chan_rows)
    gath3 = join_hi_lo(recv3_all[:, n_mix:])
    outer_tok = (
        recv3[..., :chan_rows].transpose(3, 1, 0, 2).reshape(chan_rows, tok_cols).astype(jnp.float32)
    )
    d_rows = recv3[..., chan_rows:].transpose(1, 0, 2, 3).reshape(
        blocks_here, n_seq * k_here, chan_rows
    )
    pooled = gath3[:, :n_a].reshape(n_doc, lat)
    per_doc = (
        gath3[:, n_a : n_a + n_b].reshape(n_seq, chan_rows, docs_here).transpose(1, 0, 2)
    ).reshape(chan_rows, n_doc)
    xdoc = (
        gath3[:, n_a + n_b : n_a + 2 * n_b].reshape(n_seq, chan_rows, docs_here).transpose(1, 0, 2)
    ).reshape(chan_rows, n_doc)
    g_gath = gath3[:, n_a + 2 * n_b :].reshape(1, n_doc * lat)

    spread = jnp.einsum("dl,cl->cd", pooled, up_float, precision=HIGHEST)
    summary = jnp.dot(spread, member, precision=HIGHEST)
    mixed = outer_tok + summary
    hidden = (act * mixed).astype(jnp.bfloat16)
    d_gate_bf = (upstream * mixed * sig * (1.0 + gate_pre * (1.0 - sig))).astype(jnp.bfloat16)

    d_value_bf = (
        jnp.einsum("ikj,ikc->cij", first_factor, d_rows, preferred_element_type=jnp.float32)
        .astype(jnp.bfloat16)
        .reshape(chan_rows, tok_cols)
    )
    d_first_part = jnp.einsum("ikc,cij->ikj", d_rows, blocked, preferred_element_type=jnp.float32)
    d_up = jnp.einsum("cd,dl->cl", per_doc, pooled, precision=HIGHEST)

    both_grads = jnp.concatenate([d_gate_bf, d_value_bf], axis=0)
    d_proj_part = jnp.einsum("ot,it->oi", both_grads, gathered, preferred_element_type=jnp.float32)
    rows_here = 2 * chan_rows // n_seq
    width = d_proj_part.shape[1]

    proj_send = d_proj_part.reshape(n_seq, rows_here, width).astype(jnp.bfloat16)
    proj_red = jnp.sum(seq_exchange(proj_send).astype(jnp.float32), axis=0)
    k_part = block_width // n_chan
    m_part = n_blk2 // n_chan
    first_send = (
        d_first_part.reshape(blocks_here, n_chan, k_part, block_width)
        .transpose(1, 0, 2, 3)
        .reshape(n_chan, -1)
    )
    second_send = (
        d_second_part.reshape(k_here, n_chan, m_part, n_blk2).transpose(1, 0, 2, 3).reshape(n_chan, -1)
    )
    g_send = jnp.broadcast_to(g_gath, (n_chan, n_doc * lat))
    fac_send = jnp.concatenate([first_send, second_send, g_send], axis=1)
    fac_red = lax.psum_scatter(fac_send.reshape(-1, 128), "chan", scatter_dimension=0, tiled=True)
    proj_bf = proj_red.astype(jnp.bfloat16)
    gath5 = seq_exchange(jnp.broadcast_to(proj_bf[None], (n_seq, rows_here, width)))
    d_first, d_second, d_down = epilogue(
        fac_red,
        xdoc,
        len_scale.reshape(n_doc, 1),
        (blocks_here, k_part, block_width),
        (k_here, m_part, n_blk2),
    )
    d_gate_w, d_value_w = proj_unpack(gath5)
    return (hidden, d_gate_w, d_value_w, d_first, d_second, d_down, d_up)


def solution(mesh):
    in_specs = (
        P("chan", "seq"),
        P("chan", None),
        P("chan", None),
        P("seq", None, None),
        P("seq", None, None),
        P("chan", None),
        P("chan", None),
        P(),
        P("chan", "seq"),
    )
    out_specs = (
        P("chan", "seq"),
        P("chan", None),
        P("chan", None),
        P("seq", "chan", None),
        P("seq", "chan", None),
        P("chan", None),
        P("chan", None),
    )

    return jax.shard_map(body, mesh=mesh, in_specs=in_specs, out_specs=out_specs, check_vma=False)
```

```python
import jax
import jax.numpy as jnp
from jax import lax
from jax.sharding import PartitionSpec as P
from jax.experimental import pallas as pl
from jax.experimental.pallas import tpu as pltpu


HIGHEST = lax.Precision.HIGHEST


def seq_exchange(x):
    return lax.all_to_all(x, "seq", 0, 0, tiled=True)


def split_hi_lo(x):
    hi = lax.reduce_precision(x, exponent_bits=8, mantissa_bits=7)
    lo = x - hi
    return jnp.concatenate([hi.astype(jnp.bfloat16), lo.astype(jnp.bfloat16)], axis=-1)


def join_hi_lo(x):
    n = x.shape[-1] // 2
    return x[..., :n].astype(jnp.float32) + x[..., n:].astype(jnp.float32)


def epilogue_kernel(fac_ref, xdoc_ref, scale_ref, first_ref, second_ref, down_ref):
    blocks, kp, width = first_ref.shape
    k_here, m_part, nb2 = second_ref.shape
    lanes = fac_ref.shape[1]
    rows_first = blocks * kp * width // lanes
    per_row = width // lanes
    for i in range(blocks):
        for h in range(per_row):
            first_ref[i, :, pl.ds(h * lanes, lanes)] = fac_ref[pl.ds(i * kp * per_row + h, kp, stride=per_row), :]
    rows_second = k_here * m_part * nb2 // lanes
    per_lane_row = lanes // nb2
    for k in range(k_here):
        for m in range(m_part):
            r = rows_first + (k * m_part + m) // per_lane_row
            off = (m % per_lane_row) * nb2
            second_ref[k, pl.ds(m, 1), :] = fac_ref[pl.ds(r, 1), pl.ds(off, nb2)]
    g0 = rows_first + rows_second
    g = fac_ref[pl.ds(g0, fac_ref.shape[0] - g0), :]
    dp = lax.reduce_precision(g * scale_ref[...], exponent_bits=8, mantissa_bits=7)
    down_ref[...] = jnp.dot(xdoc_ref[...], dp, precision=HIGHEST, preferred_element_type=jnp.float32)


def epilogue(fac, xdoc, scale_col, first_shape, second_shape):
    f32 = jnp.float32
    vmem = pl.BlockSpec(memory_space=pltpu.VMEM)
    return pl.pallas_call(
        epilogue_kernel,
        out_shape=(jax.ShapeDtypeStruct(first_shape, f32), jax.ShapeDtypeStruct(second_shape, f32),
                   jax.ShapeDtypeStruct((xdoc.shape[0], fac.shape[1]), f32)),
        in_specs=[vmem] * 3,
        out_specs=[vmem] * 3,
        cost_estimate=pl.CostEstimate(
            flops=2 * xdoc.shape[0] * xdoc.shape[1] * fac.shape[1] * 6,
            bytes_accessed=4 * (2 * fac.size + xdoc.size + xdoc.shape[0] * fac.shape[1]),
            transcendentals=0,
        ),
    )(fac, xdoc, scale_col)


def body(
    tokens,
    gate_weight,
    value_weight,
    first_factor,
    second_factor,
    down_latent,
    up_latent,
    doc_lengths,
    cotangent,
):
    n_seq = lax.axis_size("seq")
    n_chan = lax.axis_size("chan")
    chan_rows, tok_cols = tokens.shape
    blocks_here, block_width, _ = first_factor.shape
    k_here, n_blk2, _ = second_factor.shape
    lat = down_latent.shape[1]
    n_doc = doc_lengths.shape[0]
    docs_here = n_doc // n_seq
    me = lax.axis_index("seq")

    packed = jnp.concatenate([tokens, down_latent], axis=1)
    gathered_all = lax.all_gather(packed, "chan", axis=0, tiled=True)
    gathered = gathered_all[:, :tok_cols]
    down_full = gathered_all[:, tok_cols:]

    doc_ends = jnp.cumsum(doc_lengths)
    doc_begins = doc_ends - doc_lengths
    position = me * tok_cols + jnp.arange(tok_cols, dtype=jnp.int32)
    member = (
        (position[None, :] >= doc_begins[:, None]) & (position[None, :] < doc_ends[:, None])
    ).astype(jnp.float32)
    len_scale = lax.rsqrt(doc_lengths.astype(jnp.float32))

    gate_pre = jnp.dot(gate_weight, gathered, preferred_element_type=jnp.float32)
    value_bf = jnp.dot(value_weight, gathered, preferred_element_type=jnp.float32).astype(
        jnp.bfloat16
    )
    latent = jnp.einsum("ct,cl->lt", gathered, down_full, preferred_element_type=jnp.float32)
    doc_lat_part = jnp.einsum("dt,lt->dl", member, latent, precision=HIGHEST)
    xdoc_part = jnp.einsum(
        "ct,dt->cd", tokens, member.astype(jnp.bfloat16), preferred_element_type=jnp.float32
    )

    blocked = value_bf.reshape(chan_rows, blocks_here, block_width)
    inner_mix = jnp.einsum(
        "ikj,cij->ikc", first_factor, blocked, preferred_element_type=jnp.float32
    ).astype(jnp.bfloat16)

    sig = jax.nn.sigmoid(gate_pre)
    act = gate_pre * sig
    upstream = cotangent.astype(jnp.float32)
    d_mixed = upstream * act
    d_mixed_bf = d_mixed.astype(jnp.bfloat16)
    per_doc_part = jnp.einsum("ct,dt->cd", d_mixed, member, precision=HIGHEST)

    inner_send = inner_mix.reshape(blocks_here, n_seq, k_here, chan_rows).transpose(1, 0, 2, 3)
    d_send = d_mixed_bf.reshape(chan_rows, blocks_here, n_seq, k_here).transpose(2, 1, 3, 0)
    mix_send = jnp.concatenate([inner_send, d_send], axis=3).reshape(n_seq, -1)
    n_mix = mix_send.shape[1]

    small_send = jnp.concatenate(
        [
            doc_lat_part.reshape(n_seq, docs_here * lat),
            per_doc_part.reshape(chan_rows, n_seq, docs_here)
            .transpose(1, 0, 2)
            .reshape(n_seq, chan_rows * docs_here),
            xdoc_part.reshape(chan_rows, n_seq, docs_here)
            .transpose(1, 0, 2)
            .reshape(n_seq, chan_rows * docs_here),
        ],
        axis=1,
    )
    recv2 = seq_exchange(jnp.concatenate([mix_send, split_hi_lo(small_send)], axis=1))
    mix2 = recv2[:, :n_mix].reshape(n_seq, blocks_here, k_here, 2 * chan_rows)
    columns = mix2[..., :chan_rows].reshape(n_seq * blocks_here, k_here, chan_rows)
    d_outer = mix2[..., chan_rows:].reshape(n_seq * blocks_here, k_here, chan_rows)
    small_red = jnp.sum(join_hi_lo(recv2[:, n_mix:]), axis=0)
    n_a = docs_here * lat
    n_b = chan_rows * docs_here
    scale_here = lax.dynamic_slice(len_scale, (me * docs_here,), (docs_here,))
    pooled_here = small_red[:n_a].reshape(docs_here, lat) * scale_here[:, None]
    per_doc_here = small_red[n_a : n_a + n_b].reshape(chan_rows, docs_here)
    xdoc_here = small_red[n_a + n_b :].reshape(chan_rows, docs_here)

    up_float = up_latent.astype(jnp.float32)
    g_part = jnp.einsum("cd,cl->dl", per_doc_here, up_float, precision=HIGHEST)

    outer_mix = jnp.einsum(
        "kmi,ikc->mkc", second_factor, columns, preferred_element_type=jnp.float32
    ).astype(jnp.bfloat16)
    d_inner = jnp.einsum(
        "kmi,mkc->ikc", second_factor, d_outer, preferred_element_type=jnp.float32
    ).astype(jnp.bfloat16)
    d_second_part = jnp.einsum(
        "mkc,ikc->kmi", d_outer, columns, preferred_element_type=jnp.float32
    )

    outer_send = outer_mix.reshape(n_seq, blocks_here, k_here, chan_rows)
    dinner_send = d_inner.reshape(n_seq, blocks_here, k_here, chan_rows)
    piece = jnp.concatenate(
        [
            pooled_here.reshape(n_a),
            per_doc_here.reshape(n_b),
            xdoc_here.reshape(n_b),
            g_part.reshape(n_a),
        ]
    )
    piece_b = jnp.broadcast_to(split_hi_lo(piece)[None, :], (n_seq, 2 * piece.shape[0]))
    send3 = jnp.concatenate(
        [jnp.concatenate([outer_send, dinner_send], axis=3).reshape(n_seq, -1), piece_b], axis=1
    )
    recv3_all = seq_exchange(send3)
    recv3 = recv3_all[:, :n_mix].reshape(n_seq, blocks_here, k_here, 2 * chan_rows)
    gath3 = join_hi_lo(recv3_all[:, n_mix:])
    outer_tok = (
        recv3[..., :chan_rows].transpose(3, 1, 0, 2).reshape(chan_rows, tok_cols).astype(jnp.float32)
    )
    d_rows = recv3[..., chan_rows:].transpose(1, 0, 2, 3).reshape(
        blocks_here, n_seq * k_here, chan_rows
    )
    pooled = gath3[:, :n_a].reshape(n_doc, lat)
    per_doc = (
        gath3[:, n_a : n_a + n_b].reshape(n_seq, chan_rows, docs_here).transpose(1, 0, 2)
    ).reshape(chan_rows, n_doc)
    xdoc = (
        gath3[:, n_a + n_b : n_a + 2 * n_b].reshape(n_seq, chan_rows, docs_here).transpose(1, 0, 2)
    ).reshape(chan_rows, n_doc)
    g_gath = gath3[:, n_a + 2 * n_b :].reshape(1, n_doc * lat)

    spread = jnp.einsum("dl,cl->cd", pooled, up_float, precision=HIGHEST)
    summary = jnp.dot(spread, member, precision=HIGHEST)
    mixed = outer_tok + summary
    hidden = (act * mixed).astype(jnp.bfloat16)
    d_gate_bf = (upstream * mixed * sig * (1.0 + gate_pre * (1.0 - sig))).astype(jnp.bfloat16)

    d_value_bf = (
        jnp.einsum("ikj,ikc->cij", first_factor, d_rows, preferred_element_type=jnp.float32)
        .astype(jnp.bfloat16)
        .reshape(chan_rows, tok_cols)
    )
    d_first_part = jnp.einsum("ikc,cij->ikj", d_rows, blocked, preferred_element_type=jnp.float32)
    d_up = jnp.einsum("cd,dl->cl", per_doc, pooled, precision=HIGHEST)

    both_grads = jnp.concatenate([d_gate_bf, d_value_bf], axis=0)
    d_proj_part = jnp.einsum("ot,it->oi", both_grads, gathered, preferred_element_type=jnp.float32)
    rows_here = 2 * chan_rows // n_seq
    width = d_proj_part.shape[1]

    proj_send = d_proj_part.reshape(n_seq, rows_here, width).astype(jnp.bfloat16)
    proj_red = jnp.sum(seq_exchange(proj_send).astype(jnp.float32), axis=0)
    k_part = block_width // n_chan
    m_part = n_blk2 // n_chan
    first_send = (
        d_first_part.reshape(blocks_here, n_chan, k_part, block_width)
        .transpose(1, 0, 2, 3)
        .reshape(n_chan, -1)
    )
    second_send = (
        d_second_part.reshape(k_here, n_chan, m_part, n_blk2).transpose(1, 0, 2, 3).reshape(n_chan, -1)
    )
    g_send = jnp.broadcast_to(g_gath, (n_chan, n_doc * lat))
    fac_send = jnp.concatenate(
        [p.reshape(n_chan, -1, 128) for p in (first_send, second_send, g_send)], axis=1
    )
    fac_red = lax.psum_scatter(fac_send.reshape(-1, 128), "chan", scatter_dimension=0, tiled=True)
    proj_bf = proj_red.astype(jnp.bfloat16)
    gath5 = seq_exchange(jnp.broadcast_to(proj_bf[None], (n_seq, rows_here, width)))
    d_first, d_second, d_down = epilogue(
        fac_red,
        xdoc,
        len_scale.reshape(n_doc, 1),
        (blocks_here, k_part, block_width),
        (k_here, m_part, n_blk2),
    )
    d_proj = gath5.reshape(2 * chan_rows, width).astype(jnp.float32)
    return (hidden, d_proj[:chan_rows], d_proj[chan_rows:], d_first, d_second, d_down, d_up)


def solution(mesh):
    in_specs = (
        P("chan", "seq"),
        P("chan", None),
        P("chan", None),
        P("seq", None, None),
        P("seq", None, None),
        P("chan", None),
        P("chan", None),
        P(),
        P("chan", "seq"),
    )
    out_specs = (
        P("chan", "seq"),
        P("chan", None),
        P("chan", None),
        P("seq", "chan", None),
        P("seq", "chan", None),
        P("chan", None),
        P("chan", None),
    )

    return jax.shard_map(body, mesh=mesh, in_specs=in_specs, out_specs=out_specs, check_vma=False)
```
